32 devices in a mesh: visit: 8 (over z, y), tile: 4 (over x, core).
Axes of the slice: x: 2, y: 2, z: 4, core: 2. Of those that a mesh axis runs over, the one named last changes fastest.
Arguments:
- science: float32 [8, 256, 4096], P('visit', 'tile'), may hold values from -8 to 8
- science_var: float32 [8, 256, 4096], P('visit', 'tile'), may hold values from 0.5 to 4
- template: float32 [8, 256, 4096], P('visit', 'tile'), may hold values from -8 to 8
- template_var: float32 [8, 256, 4096], P('visit', 'tile'), may hold values from 0.1 to 1
- intersection: int32 [8, 32, 1], replicated, may hold values from 0 to 7; in each aligned block of 32 rows (0 to 31, 32 to 63, ..., all dimensions but the last counted through in order) at most 4 rows name the same one
- col_offset: int32 [8, 32], replicated, may hold values from 0 to 3968
- basis_row: float32 [16, 41], replicated, may hold values from -1 to 1
- basis_col: float32 [16, 41], replicated, may hold values from -1 to 1
- coef_sets: float32 [8, 16], replicated, may hold values from -1.5 to 1.5
- tile_coef: int32 [8, 4], replicated, may hold values from 0 to 7
Outputs:
- difference: float32 [8, 256, 4096], P('visit', 'tile')
- difference_var: float32 [8, 256, 4096], P('visit', 'tile')
The draws below stay inside these ranges and needn't reach their ends.
Inputs may be any that keep to these rules, and one draw needn't show every extreme that they name: `intersection`: no visit takes more than 4 of its 32 pieces from one owner, and some visit takes exactly 4 from one owner.
All inputs are finite; a program needn't handle non-finite values.
Results may differ from the reference program's by a relative error of at most 0.0003.
Values sent between devices are 32-bit elements; how exact they have to be, the bound alone decides.
No kernel may reach another device: no remote copies, remote signals or barrier semaphores. Data moves between devices by JAX's collectives and lax.ppermute only.
A program may use at most 320 MiB of HBM per device.

```python
import math
import jax
import jax.numpy as jnp
import numpy as np
from jax import lax

TR = 64
PIECE = 128
KP = 32
KW = 41
NB = 16
NSETS = 8
CAP = 4
VISITS = 8
TILES = 4
HEIGHT = 256
WIDTH = 4096
N_VISIT = 8


def with_ends(result, stream_key, least, top_value):
    place = [jax.random.randint(jax.random.fold_in(stream_key, axis), (), 0, length) for axis, length in enumerate(result.shape)]
    main_axis = result.shape.index(max(result.shape))
    beside = place[:main_axis] + [(place[main_axis] + 1) % result.shape[main_axis]] + place[main_axis + 1:]
    return result.at[tuple(place)].set(least).at[tuple(beside)].set(top_value)


def levels(key, extent, cuts, smallest, high):
    loudness = 1.0
    for position, blocks in cuts:
        draws = jax.random.uniform(jax.random.fold_in(jax.random.fold_in(key, 6), position), (blocks,), jnp.float32, smallest / len(cuts), high / len(cuts))
        loudness = loudness * jnp.repeat(jnp.exp(draws), extent[position] // blocks).reshape((-1,) + (1,) * (len(extent) - 1 - position))
    return loudness


def shared_out(stream_key, own, number, rows, count, top, reach, slope):
    ranking = jax.random.permutation(stream_key, count)
    packed, common = load_shares(count, rows * top, reach, slope, True), load_shares(count, rows * top, reach, slope, False)
    places = jnp.arange(count)

    def named(tallies, offset_by):
        used = int((tallies > 0).sum())
        fixed = max(1, used // 4)
        passed = fixed + (places - fixed + offset_by * (used - fixed)) % max(1, count - fixed)
        return jnp.zeros((count,), jnp.int32).at[ranking[jnp.where(places < fixed, places, passed)]].set(jnp.asarray(tallies, jnp.int32))

    tallies = jnp.where(number % 4 == 0, named(packed, number // 4), named(common, number - number // 4 - 1))
    mixed = jax.random.permutation(jax.random.fold_in(own, 3), count)
    giver, sink = mixed[0:count // 2 * 2:2], mixed[1:count // 2 * 2:2]
    slack = jnp.minimum(tallies[giver] - 1, reach - tallies[sink]) // 2
    slack = jnp.where((giver == ranking[0]) | (sink == ranking[0]) | (tallies[sink] == 0), 0, jnp.maximum(slack, 0))
    passed = jax.random.randint(jax.random.fold_in(own, 4), (count // 2,), 0, 1 << 20) % (slack + 1)
    tallies = tallies.at[giver].add(-passed).at[sink].add(passed)
    items = jnp.searchsorted(jnp.cumsum(tallies), jnp.arange(rows * top), side="right").astype(jnp.int32)
    listing = items.reshape(top, rows).T
    listing = listing[jax.random.permutation(jax.random.fold_in(own, 1), rows)]
    offset_by = jax.random.randint(jax.random.fold_in(own, 2), (rows, 1), 0, top)
    return jnp.take_along_axis(listing, (jnp.arange(top)[None, :] + offset_by) % top, axis=1)


def load_shares(count, total, reach, skew, full):
    portions = [(1 << 20) // math.isqrt(standing ** skew) + 1 for standing in range(1, count + 1)]
    largest = reach if full else min(reach, max(-(-total // count), total * portions[0] // sum(portions)))
    least = 1 if total - largest >= count - 1 else 0
    counts, spare = [largest] + [least] * (count - 1), total - largest - least * (count - 1)
    while spare > 0:
        movable = [i for i in range(1, count) if counts[i] < largest] or [i for i in range(1, count) if counts[i] < reach]
        whole, budget = sum([portions[i] for i in movable]), spare
        for i in movable:
            extra = min(reach - counts[i], max(1, budget * portions[i] // whole), spare)
            counts[i] = counts[i] + extra
            spare = spare - extra
    return np.array(counts)


def scatter_about(own_key, dims, deviation, bound, split=(), kind=jnp.bfloat16):
    entries = deviation * jax.random.normal(own_key, dims, jnp.float32)
    if split:
        entries = entries * levels(own_key, dims, split, -0.22, 0.18)
    return jnp.clip(entries, -bound, bound).astype(kind)


def setup_inputs(seed: int = 0) -> dict:
    key_of = jax.random.split(jax.random.key(seed), 11)
    science = scatter_about(key_of[0], (VISITS, HEIGHT, WIDTH), 1.0, 8.0, ((0, 8), (1, 4)), jnp.float32)
    science_var = jnp.clip(jnp.exp(math.log(4.0) - 2.0794415 * jax.random.uniform(key_of[1], (VISITS, HEIGHT, WIDTH), jnp.float32) ** levels(key_of[1], (VISITS, HEIGHT, WIDTH), ((0, 8), (1, 4)), -0.2, 0.2)), 0.5, 4.0)
    template = scatter_about(key_of[2], (VISITS, HEIGHT, WIDTH), 1.0, 8.0, ((0, 8), (1, 4)), jnp.float32)
    template_var = jnp.clip(jnp.exp(math.log(1.0) - 2.3025851 * jax.random.uniform(key_of[3], (VISITS, HEIGHT, WIDTH), jnp.float32) ** levels(key_of[3], (VISITS, HEIGHT, WIDTH), ((0, 8), (1, 4)), -0.2, 0.2)), 0.1, 1.0)
    intersection_keys = jax.random.split(jax.random.fold_in(key_of[4], 1), VISITS * KP // KP)
    intersection_turns = jax.random.permutation(jax.random.fold_in(key_of[4], 3), VISITS * KP // KP)
    intersection = jax.vmap(lambda own, number: shared_out(jax.random.fold_in(key_of[4], 2), own, number, KP, N_VISIT, 1, CAP, 2))(intersection_keys, intersection_turns).reshape((VISITS, KP, 1))
    col_offset = with_ends(jax.random.randint(key_of[5], (VISITS, KP), 0, KP * PIECE - PIECE + 1), jax.random.fold_in(key_of[5], 1), 0, KP * PIECE - PIECE).astype(jnp.int32)
    basis_row = scatter_about(key_of[6], (NB, KW), KW ** -0.5, 1.0, (), jnp.float32)
    basis_col = scatter_about(key_of[7], (NB, KW), KW ** -0.5, 1.0, (), jnp.float32)
    coef_sets = scatter_about(key_of[8], (NSETS, NB), NB ** -0.5, 1.5, (), jnp.float32)
    tile_coef = with_ends(jax.random.randint(key_of[9], (VISITS, TILES), 0, NSETS), jax.random.fold_in(key_of[9], 1), 0, NSETS - 1).astype(jnp.int32)
    return dict(science=science, science_var=science_var, template=template, template_var=template_var, intersection=intersection, col_offset=col_offset, basis_row=basis_row, basis_col=basis_col, coef_sets=coef_sets, tile_coef=tile_coef)


def reference(science, science_var, template, template_var, intersection, col_offset, basis_row, basis_col, coef_sets, tile_coef):
    margin = (KW - 1) // 2
    kernel_sets = jnp.einsum("sb,ba,bc->sac", coef_sets, basis_row, basis_col, precision=lax.Precision.HIGHEST)
    power_sets = jnp.sum(kernel_sets * kernel_sets, axis=(1, 2))
    zero_index = jnp.zeros((), jnp.int32)

    def one_visit(visit_index):
        owners = intersection[visit_index, :, 0].astype(jnp.int32)
        offsets = col_offset[visit_index].astype(jnp.int32)

        def cut_piece(owner, offset):
            fluxes = lax.dynamic_slice(template, (owner, zero_index, offset), (1, HEIGHT, PIECE))[0]
            spread = lax.dynamic_slice(template_var, (owner, zero_index, offset), (1, HEIGHT, PIECE))[0]
            return fluxes, spread

        pieces, pieces_var = jax.vmap(cut_piece)(owners, offsets)
        assembled = pieces.transpose(1, 0, 2).reshape(HEIGHT, WIDTH)
        assembled_var = pieces_var.transpose(1, 0, 2).reshape(HEIGHT, WIDTH)
        padded = jnp.pad(assembled, margin)

        def one_tile(tile_index):
            window = lax.dynamic_slice(padded, ((tile_index * TR).astype(jnp.int32), zero_index), (TR + 2 * margin, WIDTH + 2 * margin))
            chosen = tile_coef[visit_index, tile_index]
            kernel = kernel_sets[chosen]
            matched = lax.conv_general_dilated(window[None, None], kernel[None, None], (1, 1), "VALID", precision=lax.Precision.HIGHEST)[0, 0]
            return matched, power_sets[chosen]

        matched_all, powers = lax.map(one_tile, jnp.arange(TILES, dtype=jnp.int32))
        convolved = matched_all.reshape(HEIGHT, WIDTH)
        power_rows = jnp.repeat(powers, TR)
        difference = science[visit_index] - convolved
        difference_var = science_var[visit_index] + power_rows[:, None] * assembled_var
        return difference, difference_var

    difference, difference_var = lax.map(one_visit, jnp.arange(VISITS, dtype=jnp.int32))
    return difference, difference_var
```

```python
import functools

import jax
import jax.numpy as jnp
from jax import lax
from jax.experimental import pallas as pl
from jax.experimental.pallas import tpu as pltpu
from jax.sharding import PartitionSpec as P

PIECE = 128
GROUP = 7
BLOCK = 256


SMEM = pltpu.MemorySpace.SMEM
VMEM = pltpu.MemorySpace.VMEM


def partner(me, step, count):
    if count & (count - 1) == 0:
        return me ^ step
    return lax.rem(me + step, count)


def sender(me, step, count):
    if count & (count - 1) == 0:
        return me ^ step
    return lax.rem(me + count - step, count)


def pairs(step, count):
    if count & (count - 1) == 0:
        return [(i, i ^ step) for i in range(count)]
    return [(i, (i + step) % count) for i in range(count)]


def cut_kernel(count, slots, pieces, me_ref, owner_ref, offset_ref, strip_ref, *rest):
    outs, starts = rest[:count], rest[count]
    me = me_ref[0]
    rows, width = strip_ref.shape
    last = width // PIECE - 1
    lane = lax.broadcasted_iota(jnp.int32, (rows, PIECE), 1)
    for step in range(count):
        visit = partner(me, step, count)
        for slot in range(slots):
            starts[slot] = 0

        def find(k, found, visit=visit):
            starts[found] = offset_ref[visit, k]
            return found + (owner_ref[visit, k] == me).astype(jnp.int32)

        lax.fori_loop(0, pieces, find, jnp.int32(0), unroll=8)
        for slot in range(slots):
            start = starts[slot]
            block = start // PIECE
            shift = lax.rem(start, PIECE)
            after = jnp.minimum(block + 1, last)
            left = strip_ref[:, pl.ds(pl.multiple_of(block * PIECE, PIECE), PIECE)]
            right = strip_ref[:, pl.ds(pl.multiple_of(after * PIECE, PIECE), PIECE)]
            back = lax.rem(PIECE - shift, PIECE)
            left = pltpu.roll(left, back, 1)
            right = pltpu.roll(right, back, 1)
            outs[step][slot] = jnp.where(lane < PIECE - shift, left, right)


def cut(me, owners, offsets, strip, count, slots):
    pieces = owners.shape[1]
    rows = strip.shape[0]
    shape = jax.ShapeDtypeStruct((slots, rows, PIECE), jnp.float32)
    return pl.pallas_call(
        functools.partial(cut_kernel, count, slots, pieces),
        out_shape=[shape] * count,
        in_specs=[pl.BlockSpec(memory_space=SMEM)] * 3 + [pl.BlockSpec(memory_space=VMEM)],
        out_specs=[pl.BlockSpec(memory_space=VMEM)] * count,
        scratch_shapes=[pltpu.SMEM((slots + 1,), jnp.int32)],
        cost_estimate=pl.CostEstimate(flops=0, transcendentals=0, bytes_accessed=2 * strip.size * 4),
        name="cut",
    )(me, owners, offsets, strip)


def find_places(count, slots, pieces, me, owner_ref, place, seen):
    for owner in range(count):
        seen[owner] = 0
    for entry in range(count * slots):
        place[entry] = -1

    def find(k, carry):
        owner = owner_ref[me, k]
        nth = seen[owner]
        place[owner * slots + nth] = k
        seen[owner] = nth + 1
        return carry

    lax.fori_loop(0, pieces, find, jnp.int32(0), unroll=4)


def each_piece(count, slots, pieces, me, place, body):
    for step in range(count):
        owner = sender(me, step, count)
        for slot in range(slots):
            k = place[owner * slots + slot]
            columns = pl.ds(pl.multiple_of(k * PIECE, PIECE), PIECE)
            if count * slots == pieces:
                body(step, slot, columns)
            else:
                pl.when(k >= 0)(functools.partial(body, step, slot, columns))


def gather_kernel(count, slots, pieces, reach, me_ref, owner_ref, *rest):
    blocks = rest[:count]
    image_ref, head_ref, tail_ref, place, seen = rest[count:]
    me = me_ref[0]
    rows = image_ref.shape[0]
    find_places(count, slots, pieces, me, owner_ref, place, seen)

    def put(step, slot, columns):
        piece = blocks[step][slot]
        image_ref[:, columns] = piece
        head_ref[:, columns] = piece[:reach]
        tail_ref[:, columns] = piece[rows - reach :]

    each_piece(count, slots, pieces, me, place, put)


def gather(me, owners, blocks, width, reach):
    count, pieces = len(blocks), owners.shape[1]
    slots, rows = blocks[0].shape[:2]
    return pl.pallas_call(
        functools.partial(gather_kernel, count, slots, pieces, reach),
        out_shape=[
            jax.ShapeDtypeStruct((rows, width), jnp.float32),
            jax.ShapeDtypeStruct((reach, width), jnp.float32),
            jax.ShapeDtypeStruct((reach, width), jnp.float32),
        ],
        in_specs=[pl.BlockSpec(memory_space=SMEM)] * 2 + [pl.BlockSpec(memory_space=VMEM)] * count,
        out_specs=[pl.BlockSpec(memory_space=VMEM)] * 3,
        scratch_shapes=[pltpu.SMEM((count * slots,), jnp.int32), pltpu.SMEM((count,), jnp.int32)],
        cost_estimate=pl.CostEstimate(flops=0, transcendentals=0, bytes_accessed=3 * rows * width * 4),
        name="gather",
    )(me, owners, *blocks)


def spread_kernel(count, slots, pieces, me_ref, owner_ref, power_ref, science_ref, *rest):
    blocks = rest[:count]
    out_ref, place, seen = rest[count:]
    me = me_ref[0]
    power = power_ref[0]
    find_places(count, slots, pieces, me, owner_ref, place, seen)

    def put(step, slot, columns):
        out_ref[:, columns] = science_ref[:, columns] + power * blocks[step][slot]

    each_piece(count, slots, pieces, me, place, put)


def spread(me, owners, power, science_var, blocks):
    count, pieces = len(blocks), owners.shape[1]
    slots = blocks[0].shape[0]
    return pl.pallas_call(
        functools.partial(spread_kernel, count, slots, pieces),
        out_shape=jax.ShapeDtypeStruct(science_var.shape, jnp.float32),
        in_specs=[pl.BlockSpec(memory_space=SMEM)] * 3 + [pl.BlockSpec(memory_space=VMEM)] * (1 + count),
        out_specs=pl.BlockSpec(memory_space=VMEM),
        scratch_shapes=[pltpu.SMEM((count * slots,), jnp.int32), pltpu.SMEM((count,), jnp.int32)],
        cost_estimate=pl.CostEstimate(flops=2 * science_var.size, transcendentals=0, bytes_accessed=3 * science_var.size * 4),
        name="spread",
    )(me, owners, power, science_var, *blocks)


def split(x):
    high = x.astype(jnp.bfloat16)
    return high, (x - high.astype(jnp.float32)).astype(jnp.bfloat16)


def band_kernel(taps, rows, lead, taps_ref, high_ref, low_ref):
    depth = taps_ref.shape[1]
    for c in range(taps):
        m, q = c // GROUP, c % GROUP
        line = jnp.broadcast_to(taps_ref[c : c + 1, :], (rows, depth))
        band = pltpu.roll(line, lead, 1, stride=1, stride_axis=0)
        high, low = split(band)
        high_ref[q * rows : (q + 1) * rows, m * depth : (m + 1) * depth] = high
        low_ref[q * rows : (q + 1) * rows, m * depth : (m + 1) * depth] = low


def bands(taps_t, rows, lead):
    taps, depth = taps_t.shape
    shape = jax.ShapeDtypeStruct((GROUP * rows, taps // GROUP * depth), jnp.bfloat16)
    return pl.pallas_call(
        functools.partial(band_kernel, taps, rows, lead),
        out_shape=[shape, shape],
        in_specs=[pl.BlockSpec(memory_space=VMEM)],
        out_specs=[pl.BlockSpec(memory_space=VMEM)] * 2,
        cost_estimate=pl.CostEstimate(flops=0, transcendentals=0, bytes_accessed=4 * shape.size),
        name="bands",
    )(taps_t)


def match_kernel(
    margin, high_ref, low_ref, image_ref, above_ref, below_ref, science_ref, out_ref, wide, z_high, z_low, partial
):
    rows, width = image_ref.shape
    reach = above_ref.shape[0]
    shifts = high_ref.shape[1] // z_depth(rows, reach)
    depth = z_depth(rows, reach)
    filled = rows + 2 * reach
    wide[:, 0:PIECE] = jnp.zeros((filled, PIECE), jnp.float32)
    wide[:, PIECE + width :] = jnp.zeros((filled, wide.shape[1] - PIECE - width), jnp.float32)
    wide[0:reach, PIECE : PIECE + width] = above_ref[...]
    wide[reach : reach + rows, PIECE : PIECE + width] = image_ref[...]
    wide[reach + rows :, PIECE : PIECE + width] = below_ref[...]
    if filled < depth:
        empty = jnp.zeros((depth - filled, BLOCK), jnp.bfloat16)
        for m in range(shifts):
            z_high[m * depth + filled : (m + 1) * depth, :] = empty
            z_low[m * depth + filled : (m + 1) * depth, :] = empty
    blocks = width // BLOCK

    def join(b):
        begin = pl.multiple_of(b * BLOCK, BLOCK)
        for half in range(BLOCK // PIECE):
            at = pl.multiple_of(begin + half * PIECE, PIECE)
            total = partial[0:rows, pl.ds(at, PIECE)]
            for q in range(1, GROUP):
                pair = partial[q * rows : (q + 1) * rows, pl.ds(at, 2 * PIECE)]
                total = total + pltpu.roll(pair, 2 * PIECE - q, 1)[:, :PIECE]
            out_ref[:, pl.ds(at, PIECE)] = science_ref[:, pl.ds(at, PIECE)] - total

    def multiply(b):
        begin = pl.multiple_of(b * BLOCK, BLOCK)
        for m in range(shifts):
            offset = PIECE - margin + m * GROUP
            base = offset // PIECE * PIECE
            window = wide[:, pl.ds(pl.multiple_of(begin + base, PIECE), BLOCK + PIECE)]
            if offset > base:
                window = pltpu.roll(window, BLOCK + PIECE - (offset - base), 1)
            high, low = split(window[:, :BLOCK])
            z_high[m * depth : m * depth + filled, :] = high
            z_low[m * depth : m * depth + filled, :] = low
        product = jnp.dot(high_ref[...], z_high[...], preferred_element_type=jnp.float32)
        product += jnp.dot(high_ref[...], z_low[...], preferred_element_type=jnp.float32)
        product += jnp.dot(low_ref[...], z_high[...], preferred_element_type=jnp.float32)
        partial[:, pl.ds(begin, BLOCK)] = product

    multiply(0)
    multiply(1)

    @pl.loop(2, blocks + 1)
    def _(b):
        join(b - 2)
        multiply(b)

    join(blocks - 1)


def z_depth(rows, reach):
    return -(-(rows + 2 * reach) // PIECE) * PIECE


def match(margin, high, low, image, above, below, science):
    rows, width = image.shape
    reach = above.shape[0]
    filled = rows + 2 * reach
    deep = high.shape[1]
    return pl.pallas_call(
        functools.partial(match_kernel, margin),
        out_shape=jax.ShapeDtypeStruct(science.shape, jnp.float32),
        in_specs=[pl.BlockSpec(memory_space=VMEM)] * 6,
        out_specs=pl.BlockSpec(memory_space=VMEM),
        scratch_shapes=[
            pltpu.VMEM((filled, width + BLOCK + 2 * PIECE), jnp.float32),
            pltpu.VMEM((deep, BLOCK), jnp.bfloat16),
            pltpu.VMEM((deep, BLOCK), jnp.bfloat16),
            pltpu.VMEM((GROUP * rows, width + BLOCK), jnp.float32),
        ],
        cost_estimate=pl.CostEstimate(
            flops=6 * GROUP * rows * deep * width, transcendentals=0, bytes_accessed=4 * rows * width * 4
        ),
        name="match",
    )(high, low, image, above, below, science)


def local(
    science,
    science_var,
    template,
    template_var,
    intersection,
    col_offset,
    basis_row,
    basis_col,
    coef_sets,
    tile_coef,
):
    count = lax.axis_size("visit")
    pieces = intersection.shape[1]
    slots = max(2, pieces // count)
    rows, width = science.shape[1:]
    side = basis_row.shape[1]
    margin = (side - 1) // 2
    reach = -(-margin // 8) * 8
    depth = z_depth(rows, reach)
    me = lax.axis_index("visit")
    tile_me = lax.axis_index("tile")
    highest = lax.Precision.HIGHEST
    me_ref = me.astype(jnp.int32).reshape(1)
    owners = intersection[:, :, 0]
    order = sorted(range(1, count), key=lambda step: -(step.bit_length()))

    mine = cut(me_ref, owners, col_offset, template[0], count, slots)
    got = [mine[0]] + [None] * (count - 1)
    for step in order:
        got[step] = lax.ppermute(mine[step], "visit", pairs(step, count))
    mine_var = cut(me_ref, owners, col_offset, template_var[0], count, slots)
    got_var = [mine_var[0]] + [None] * (count - 1)
    for step in order:
        got_var[step] = lax.ppermute(mine_var[step], "visit", pairs(step, count))

    chosen = lax.dynamic_slice(tile_coef, (me, tile_me), (1, 1))[0, 0]
    coeffs = lax.dynamic_index_in_dim(coef_sets, chosen, 0, keepdims=False)
    taps = jnp.einsum("bc,ba->ca", coeffs[:, None] * basis_col, basis_row, precision=highest)
    power = jnp.sum(taps * taps).reshape(1)
    grouped = -(-side // GROUP) * GROUP
    taps = jnp.pad(taps, ((0, grouped - side), (0, depth - side)))
    high, low = bands(taps, rows, reach - margin)

    image, head, tail = gather(me_ref, owners, got, width, reach)
    tiles = lax.axis_size("tile")
    above = lax.ppermute(tail, "tile", [(i, i + 1) for i in range(tiles - 1)])
    below = lax.ppermute(head, "tile", [(i + 1, i) for i in range(tiles - 1)])
    difference = match(margin, high, low, image, above, below, science[0])
    difference_var = spread(me_ref, owners, power, science_var[0], got_var)
    return difference[None], difference_var[None]


def solution(mesh):
    split_spec = P("visit", "tile", None)
    return jax.shard_map(
        local,
        mesh=mesh,
        in_specs=(split_spec,) * 4 + (P(),) * 6,
        out_specs=(split_spec, split_spec),
        check_vma=False,
    )
```

```python
import functools

import jax
import jax.numpy as jnp
from jax import lax
from jax.experimental import pallas as pl
from jax.experimental.pallas import tpu as pltpu
from jax.sharding import PartitionSpec as P


PIECE = 128
GROUP = 11
SUB = 16
BLOCK = 256


SMEM = pltpu.MemorySpace.SMEM
VMEM = pltpu.MemorySpace.VMEM


def partner(me, step, count):
    if count & (count - 1) == 0:
        return me ^ step
    return lax.rem(me + step, count)


def sender(me, step, count):
    if count & (count - 1) == 0:
        return me ^ step
    return lax.rem(me + count - step, count)


def pairs(step, count):
    if count & (count - 1) == 0:
        return [(i, i ^ step) for i in range(count)]
    return [(i, (i + step) % count) for i in range(count)]


def cut_kernel(count, slots, pieces, me_ref, owner_ref, offset_ref, strip_ref, *rest):
    outs, (strip, cuts, starts, strip_sem, out_sems) = rest[:count], rest[count:]
    me = me_ref[0]
    rows, width = strip.shape
    last = width // PIECE - 1
    load = pltpu.make_async_copy(strip_ref, strip, strip_sem)
    load.start()
    for step in range(count):
        visit = partner(me, step, count)
        begin = step * (slots + 1)
        for slot in range(slots):
            starts[begin + slot] = 0
        found = jnp.int32(begin)
        for k in range(pieces):
            starts[found] = offset_ref[visit, k]
            found = found + (owner_ref[visit, k] == me).astype(jnp.int32)
    load.wait()
    lane = lax.broadcasted_iota(jnp.int32, (rows, PIECE), 1)
    stores = []
    for step in range(count):
        for slot in range(slots):
            start = starts[step * (slots + 1) + slot]
            block = start // PIECE
            shift = lax.rem(start, PIECE)
            after = jnp.minimum(block + 1, last)
            left = strip[:, pl.ds(pl.multiple_of(block * PIECE, PIECE), PIECE)]
            right = strip[:, pl.ds(pl.multiple_of(after * PIECE, PIECE), PIECE)]
            joined = jnp.where(lane < shift, right, left)
            cuts[step, slot] = pltpu.roll(joined, lax.rem(PIECE - shift, PIECE), 1)
        store = pltpu.make_async_copy(cuts.at[step], outs[step], out_sems.at[step])
        store.start()
        stores.append(store)
    for store in stores:
        store.wait()


def cut(me, owners, offsets, strip, count, slots):
    pieces = owners.shape[1]
    rows, width = strip.shape
    shape = jax.ShapeDtypeStruct((slots, rows, PIECE), jnp.float32)
    return pl.pallas_call(
        functools.partial(cut_kernel, count, slots, pieces),
        out_shape=[shape] * count,
        in_specs=[pl.BlockSpec(memory_space=SMEM)] * 3 + [pl.BlockSpec(memory_space=pl.ANY)],
        out_specs=[pl.BlockSpec(memory_space=pl.ANY)] * count,
        scratch_shapes=[
            pltpu.VMEM((rows, width), jnp.float32),
            pltpu.VMEM((count, slots, rows, PIECE), jnp.float32),
            pltpu.SMEM((count * (slots + 1),), jnp.int32),
            pltpu.SemaphoreType.DMA,
            pltpu.SemaphoreType.DMA((count,)),
        ],
        cost_estimate=pl.CostEstimate(flops=0, transcendentals=0, bytes_accessed=2 * strip.size * 4),
        name="cut",
    )(me, owners, offsets, strip)


def find_places(count, slots, pieces, me, owner_ref, place, seen):
    for owner in range(count):
        seen[owner] = 0
    for entry in range(count * slots):
        place[entry] = -1

    def find(k, carry):
        owner = owner_ref[me, k]
        nth = seen[owner]
        place[owner * slots + nth] = k
        seen[owner] = nth + 1
        return carry

    lax.fori_loop(0, pieces, find, jnp.int32(0), unroll=8)


def when_taken(count, slots, pieces, k, body):
    if count * slots == pieces:
        body()
    else:
        pl.when(k >= 0)(body)


def at_piece(k):
    return pl.ds(pl.multiple_of(k * PIECE, PIECE), PIECE)


def each_slot(count, slots, me, place):
    for step in range(count):
        owner = sender(me, step, count)
        for slot in range(slots):
            yield step, slot, place[owner * slots + slot]


def places_scratch(count, slots):
    return [pltpu.SMEM((count * slots,), jnp.int32), pltpu.SMEM((count,), jnp.int32)]


def edges_kernel(count, slots, pieces, reach, me_ref, owner_ref, *rest):
    blocks = rest[:count]
    head_ref, tail_ref, place, seen = rest[count:]
    me = me_ref[0]
    rows = blocks[0].shape[1]
    find_places(count, slots, pieces, me, owner_ref, place, seen)
    for position, slot, k in each_slot(count, slots, me, place):

        def put(position=position, slot=slot, k=k):
            head_ref[:, at_piece(k)] = blocks[position][slot, :reach]
            tail_ref[:, at_piece(k)] = blocks[position][slot, rows - reach :]

        when_taken(count, slots, pieces, k, put)


def edges(me, owners, blocks, width, reach):
    count, pieces = len(blocks), owners.shape[1]
    slots = blocks[0].shape[0]
    shape = jax.ShapeDtypeStruct((reach, width), jnp.float32)
    return pl.pallas_call(
        functools.partial(edges_kernel, count, slots, pieces, reach),
        out_shape=[shape, shape],
        in_specs=[pl.BlockSpec(memory_space=SMEM)] * 2 + [pl.BlockSpec(memory_space=VMEM)] * count,
        out_specs=[pl.BlockSpec(memory_space=VMEM)] * 2,
        scratch_shapes=places_scratch(count, slots),
        cost_estimate=pl.CostEstimate(flops=0, transcendentals=0, bytes_accessed=4 * reach * width * 4),
        compiler_params=pltpu.CompilerParams(vmem_limit_bytes=6 << 20),
        name="edges",
    )(me, owners, *blocks)


def spread_kernel(count, slots, pieces, me_ref, owner_ref, power_ref, science_ref, *rest):
    blocks = rest[:count]
    out_ref, place, seen = rest[count:]
    me = me_ref[0]
    power = power_ref[0]
    find_places(count, slots, pieces, me, owner_ref, place, seen)
    for position, slot, k in each_slot(count, slots, me, place):

        def put(position=position, slot=slot, k=k):
            out_ref[:, at_piece(k)] = science_ref[:, at_piece(k)] + power * blocks[position][slot]

        when_taken(count, slots, pieces, k, put)


def spread(me, owners, power, science_var, blocks):
    count, pieces = len(blocks), owners.shape[1]
    slots = blocks[0].shape[0]
    size = science_var.size
    return pl.pallas_call(
        functools.partial(spread_kernel, count, slots, pieces),
        out_shape=jax.ShapeDtypeStruct(science_var.shape, jnp.float32),
        in_specs=[pl.BlockSpec(memory_space=SMEM)] * 3 + [pl.BlockSpec(memory_space=VMEM)] * (1 + count),
        out_specs=pl.BlockSpec(memory_space=VMEM),
        scratch_shapes=places_scratch(count, slots),
        cost_estimate=pl.CostEstimate(flops=2 * size, transcendentals=0, bytes_accessed=3 * size * 4),
        compiler_params=pltpu.CompilerParams(vmem_limit_bytes=6 << 20),
        name="spread",
    )(me, owners, power, science_var, *blocks)


def split(x):
    high = x.astype(jnp.bfloat16)
    return high, (x - high.astype(jnp.float32)).astype(jnp.bfloat16)


def band_kernel(taps_ref, both_ref):
    deep = taps_ref.shape[1]
    half = both_ref.shape[0] // 2
    for q in range(GROUP):
        for at in range(0, deep, PIECE):
            line = jnp.broadcast_to(taps_ref[q : q + 1, at : at + PIECE], (SUB, PIECE))
            high, low = split(pltpu.roll(line, 0, 1, stride=1, stride_axis=0))
            both_ref[q * SUB : (q + 1) * SUB, at : at + PIECE] = high
            both_ref[half + q * SUB : half + (q + 1) * SUB, at : at + PIECE] = low


def bands(taps, window, lead):
    side = taps.shape[0]
    shifts = -(-side // GROUP)
    taps = jnp.pad(taps, ((0, shifts * GROUP - side), (lead, window - lead - side)))
    taps = taps.reshape(shifts, GROUP, window).transpose(1, 0, 2).reshape(GROUP, shifts * window)
    deep = -(-shifts * window // PIECE) * PIECE
    taps = jnp.pad(taps, ((0, 0), (0, deep - shifts * window)))
    return pl.pallas_call(
        band_kernel,
        out_shape=jax.ShapeDtypeStruct((2 * GROUP * SUB, deep), jnp.bfloat16),
        in_specs=[pl.BlockSpec(memory_space=VMEM)],
        out_specs=pl.BlockSpec(memory_space=VMEM),
        cost_estimate=pl.CostEstimate(flops=0, transcendentals=0, bytes_accessed=4 * GROUP * SUB * deep),
        compiler_params=pltpu.CompilerParams(vmem_limit_bytes=4 << 20),
        name="bands",
    )(taps)


def turn(x, lanes):
    return pltpu.roll(x, PIECE - lanes, 1)


def match_kernel(margin, shifts, count, slots, pieces, me_ref, owner_ref, both_ref, above_ref, below_ref, science_ref, *rest):
    images, out_ref, rest = rest[:count], rest[count], rest[count + 1 :]
    place, seen, wide, high0, high1, low0, low1, part0, part1, kept_image, kept_part = rest
    rows, width = science_ref.shape
    reach = above_ref.shape[0]
    window = SUB + 2 * reach
    filled = rows + 2 * reach
    half = both_ref.shape[0] // 2
    high, low, part = (high0, high1), (low0, low1), (part0, part1)
    me = me_ref[0]
    find_places(count, slots, pieces, me, owner_ref, place, seen)
    for position, slot, k in each_slot(count, slots, me, place):

        def put(position=position, slot=slot, k=k):
            wide[reach : reach + rows, at_piece(k + 1)] = images[position][slot]

        when_taken(count, slots, pieces, k, put)
    wide[:, 0:PIECE] = jnp.zeros((filled, PIECE), jnp.float32)
    wide[:, PIECE + width :] = jnp.zeros((filled, wide.shape[1] - PIECE - width), jnp.float32)
    wide[0:reach, PIECE : PIECE + width] = above_ref[...]
    wide[reach + rows :, PIECE : PIECE + width] = below_ref[...]
    blocks = width // BLOCK
    lane_image = lax.broadcasted_iota(jnp.int32, (filled, PIECE), 1)
    lane_part = lax.broadcasted_iota(jnp.int32, (SUB, PIECE), 1)

    def build(b, parity, first=False):
        begin = b * BLOCK
        for m in range(shifts):
            offset = PIECE - margin + m * GROUP
            lanes = offset % PIECE
            at = begin + offset - lanes
            span = slice(m * filled, (m + 1) * filled)

            def column(k, at=at):
                return wide[:, pl.ds(pl.multiple_of(at + k * PIECE, PIECE), PIECE)]

            if lanes:
                turned = [turn(column(0), lanes) if first else kept_image[span, :]]
                turned += [turn(column(k), lanes) for k in (1, 2)]
                kept_image[span, :] = turned[2]
                mask = lane_image < PIECE - lanes
                parts = [jnp.where(mask, turned[k], turned[k + 1]) for k in (0, 1)]
            else:
                parts = [column(0), column(1)]
            for k in (0, 1):
                near, rest = split(parts[k])
                high[parity][span, k * PIECE : (k + 1) * PIECE] = near
                low[parity][span, k * PIECE : (k + 1) * PIECE] = rest

    def multiply(parity, columns=BLOCK):
        for top in range(0, rows, SUB):
            spans = [slice(m * filled + top, m * filled + top + window) for m in range(shifts)]
            near = jnp.concatenate([high[parity][span, :columns] for span in spans], axis=0)
            rest = jnp.concatenate([low[parity][span, :columns] for span in spans], axis=0)
            deep = near.shape[0]
            product = jnp.dot(both_ref[:half, :deep], rest, preferred_element_type=jnp.float32)
            pair = jnp.dot(both_ref[:, :deep], near, preferred_element_type=jnp.float32)
            part[parity][top * GROUP : (top + SUB) * GROUP, :columns] = product + (pair[:half] + pair[half:])

    def keep():
        for first in range(0, rows * GROUP, SUB):
            q = first // SUB % GROUP
            if q:
                kept_part[first : first + SUB, :] = turn(part0[first : first + SUB, :PIECE], q)

    def join(b, parity):
        here, after = part[parity], part[1 - parity]
        begin = pl.multiple_of(b * BLOCK, BLOCK)
        for top in range(0, rows, SUB):
            span = slice(top * GROUP, top * GROUP + SUB)
            totals = [here[span, :PIECE], here[span, PIECE:]]
            for q in range(1, GROUP):
                span = slice(top * GROUP + q * SUB, top * GROUP + (q + 1) * SUB)
                turned = [kept_part[span, :], turn(here[span, PIECE:], q), turn(after[span, :PIECE], q)]
                kept_part[span, :] = turned[2]
                for k in (0, 1):
                    totals[k] = totals[k] + jnp.where(lane_part < PIECE - q, turned[k], turned[k + 1])
            for k in (0, 1):
                at = pl.ds(pl.multiple_of(begin + k * PIECE, PIECE), PIECE)
                out_ref[top : top + SUB, at] = science_ref[top : top + SUB, at] - totals[k]

    build(0, 0, first=True)
    build(1, 1)
    multiply(0)
    keep()
    build(2, 0)
    multiply(1)

    @pl.loop(1, blocks // 2)
    def _(p):
        b = p * 2
        join(b - 2, 0)
        build(b + 1, 1)
        multiply(0)
        join(b - 1, 1)
        build(b + 2, 0)
        multiply(1)

    join(blocks - 2, 0)
    multiply(0, PIECE)
    join(blocks - 1, 1)


def match(margin, shifts, me, owners, both, above, below, science, images):
    rows, width = science.shape
    count, pieces = len(images), owners.shape[1]
    slots = images[0].shape[0]
    reach = above.shape[0]
    filled = rows + 2 * reach
    return pl.pallas_call(
        functools.partial(match_kernel, margin, shifts, count, slots, pieces),
        out_shape=jax.ShapeDtypeStruct(science.shape, jnp.float32),
        in_specs=[pl.BlockSpec(memory_space=SMEM)] * 2
        + [pl.BlockSpec(memory_space=VMEM)] * (4 + count),
        out_specs=pl.BlockSpec(memory_space=VMEM),
        scratch_shapes=places_scratch(count, slots)
        + [
            pltpu.VMEM((filled, width + BLOCK + 2 * PIECE), jnp.float32),
            *[pltpu.VMEM((shifts * filled, BLOCK), jnp.bfloat16)] * 4,
            *[pltpu.VMEM((GROUP * rows, BLOCK), jnp.float32)] * 2,
            pltpu.VMEM((shifts * filled, PIECE), jnp.float32),
            pltpu.VMEM((GROUP * rows, PIECE), jnp.float32),
        ],
        cost_estimate=pl.CostEstimate(
            flops=6 * GROUP * rows * both.shape[1] * width, transcendentals=0, bytes_accessed=4 * rows * width * 4
        ),
        compiler_params=pltpu.CompilerParams(vmem_limit_bytes=20 << 20),
        name="match",
    )(me, owners, both, above, below, science, *images)


def local(
    science,
    science_var,
    template,
    template_var,
    intersection,
    col_offset,
    basis_row,
    basis_col,
    coef_sets,
    tile_coef,
):
    count = lax.axis_size("visit")
    pieces = intersection.shape[1]
    slots = max(2, pieces // count)
    _, width = science.shape[1:]
    side = basis_row.shape[1]
    margin = (side - 1) // 2
    reach = -(-margin // 8) * 8
    me = lax.axis_index("visit")
    tile_me = lax.axis_index("tile")
    highest = lax.Precision.HIGHEST
    me_ref = me.astype(jnp.int32).reshape(1)
    owners = intersection[:, :, 0]
    mine = cut(me_ref, owners, col_offset, template[0], count, slots)
    got = [mine[0]] + [None] * (count - 1)
    for step in steps(count):
        got[step] = lax.ppermute(mine[step], "visit", pairs(step, count))
    mine_var = cut(me_ref, owners, col_offset, template_var[0], count, slots)
    got_var = [mine_var[0]] + [None] * (count - 1)
    for step in steps(count):
        got_var[step] = lax.ppermute(mine_var[step], "visit", pairs(step, count))

    chosen = lax.dynamic_slice(tile_coef, (me, tile_me), (1, 1))[0, 0]
    coeffs = lax.dynamic_index_in_dim(coef_sets, chosen, 0, keepdims=False)
    taps = jnp.einsum("bc,ba->ca", coeffs[:, None] * basis_col, basis_row, precision=highest)
    power = jnp.sum(taps * taps).reshape(1)
    both = bands(taps, SUB + 2 * reach, reach - margin)

    head, tail = edges(me_ref, owners, got, width, reach)
    tiles = lax.axis_size("tile")
    above = lax.ppermute(tail, "tile", [(i, i + 1) for i in range(tiles - 1)])
    below = lax.ppermute(head, "tile", [(i + 1, i) for i in range(tiles - 1)])
    shifts = -(-side // GROUP)
    difference = match(margin, shifts, me_ref, owners, both, above, below, science[0], got)
    difference_var = spread(me_ref, owners, power, science_var[0], got_var)
    return difference[None], difference_var[None]


def steps(count):
    return sorted(range(1, count), key=lambda step: -(step.bit_length()))


def solution(mesh):
    split_spec = P("visit", "tile", None)
    return jax.shard_map(
        local,
        mesh=mesh,
        in_specs=(split_spec,) * 4 + (P(),) * 6,
        out_specs=(split_spec, split_spec),
        check_vma=False,
    )
```

```python
import functools

import jax
import jax.numpy as jnp
from jax import lax
from jax.experimental import pallas as pl
from jax.experimental.pallas import tpu as pltpu
from jax.sharding import PartitionSpec as P


PIECE = 128
GROUP = 11
SUB = 16
BLOCK = 256


SMEM = pltpu.MemorySpace.SMEM
VMEM = pltpu.MemorySpace.VMEM
HBM = pltpu.MemorySpace.HBM


def partner(me, step, count):
    if count & (count - 1) == 0:
        return me ^ step
    return lax.rem(me + step, count)


def sender(me, step, count):
    if count & (count - 1) == 0:
        return me ^ step
    return lax.rem(me + count - step, count)


def pairs(step, count):
    if count & (count - 1) == 0:
        return [(i, i ^ step) for i in range(count)]
    return [(i, (i + step) % count) for i in range(count)]


def cut_kernel(count, slots, pieces, owner_hbm, offset_hbm, strip_hbm, *rest):
    outs, (strip, owner_ref, offset_ref, starts, sems) = rest[:count], rest[count:]
    me = lax.axis_index("visit")
    rows, width = strip.shape
    last = width // PIECE - 1
    loads = [
        pltpu.make_async_copy(source, target, sems.at[i])
        for i, (source, target) in enumerate(((owner_hbm, owner_ref), (offset_hbm, offset_ref), (strip_hbm, strip)))
    ]
    for load in loads:
        load.start()
    for load in loads[:2]:
        load.wait()
    for step in range(count):
        visit = partner(me, step, count)
        begin = step * (slots + 1)
        for slot in range(slots):
            starts[begin + slot] = 0
        found = jnp.int32(begin)
        for k in range(pieces):
            starts[found] = offset_ref[visit, k]
            found = found + (owner_ref[visit, k] == me).astype(jnp.int32)
    loads[2].wait()
    lane = lax.broadcasted_iota(jnp.int32, (rows, PIECE), 1)
    for step in range(count):
        for slot in range(slots):
            start = starts[step * (slots + 1) + slot]
            block = start // PIECE
            shift = lax.rem(start, PIECE)
            after = jnp.minimum(block + 1, last)
            left = strip[:, pl.ds(pl.multiple_of(block * PIECE, PIECE), PIECE)]
            right = strip[:, pl.ds(pl.multiple_of(after * PIECE, PIECE), PIECE)]
            joined = jnp.where(lane < shift, right, left)
            outs[step][slot] = pltpu.roll(joined, lax.rem(PIECE - shift, PIECE), 1)


def cut(owners, offsets, strip, count, slots):
    rows, width = strip.shape
    shape = jax.ShapeDtypeStruct((slots, rows, PIECE), jnp.float32)
    return pl.pallas_call(
        functools.partial(cut_kernel, count, slots, owners.shape[1]),
        out_shape=[shape] * count,
        in_specs=[pl.BlockSpec(memory_space=HBM)] * 3,
        out_specs=[pl.BlockSpec(memory_space=VMEM)] * count,
        scratch_shapes=[
            pltpu.VMEM((rows, width), jnp.float32),
            pltpu.SMEM(owners.shape, jnp.int32),
            pltpu.SMEM(offsets.shape, jnp.int32),
            pltpu.SMEM((count * (slots + 1),), jnp.int32),
            pltpu.SemaphoreType.DMA((3,)),
        ],
        cost_estimate=pl.CostEstimate(flops=0, transcendentals=0, bytes_accessed=2 * strip.size * 4),
        name="cut",
    )(owners, offsets, strip)


def find_places(count, slots, pieces, me, owner_ref, place, seen):
    for owner in range(count):
        seen[owner] = 0
    for entry in range(count * slots):
        place[entry] = -1

    def find(k, carry):
        owner = owner_ref[me, k]
        nth = seen[owner]
        place[owner * slots + nth] = k
        seen[owner] = nth + 1
        return carry

    lax.fori_loop(0, pieces, find, jnp.int32(0), unroll=8)


def when_taken(count, slots, pieces, k, body):
    if count * slots == pieces:
        body()
    else:
        pl.when(k >= 0)(body)


def at_piece(k):
    return pl.ds(pl.multiple_of(k * PIECE, PIECE), PIECE)


def each_slot(count, slots, me, place, steps):
    number = 0
    for position, step in enumerate(steps):
        owner = sender(me, step, count)
        for slot in range(slots):
            yield number, position, slot, place[owner * slots + slot]
            number += 1


def places_scratch(count, slots):
    return [pltpu.SMEM((count * slots,), jnp.int32), pltpu.SMEM((count,), jnp.int32)]


def edges_kernel(count, slots, pieces, reach, owner_ref, *rest):
    blocks = rest[:count]
    head_ref, tail_ref, place, seen = rest[count:]
    me = lax.axis_index("visit")
    rows = blocks[0].shape[1]
    find_places(count, slots, pieces, me, owner_ref, place, seen)
    for _, position, slot, k in each_slot(count, slots, me, place, range(count)):

        def put(position=position, slot=slot, k=k):
            head_ref[:, at_piece(k)] = blocks[position][slot, :reach]
            tail_ref[:, at_piece(k)] = blocks[position][slot, rows - reach :]

        when_taken(count, slots, pieces, k, put)


def edges(owners, blocks, width, reach):
    count, pieces = len(blocks), owners.shape[1]
    slots = blocks[0].shape[0]
    shape = jax.ShapeDtypeStruct((reach, width), jnp.float32)
    return pl.pallas_call(
        functools.partial(edges_kernel, count, slots, pieces, reach),
        out_shape=[shape, shape],
        in_specs=[pl.BlockSpec(memory_space=SMEM)] + [pl.BlockSpec(memory_space=VMEM)] * count,
        out_specs=[pl.BlockSpec(memory_space=VMEM)] * 2,
        scratch_shapes=places_scratch(count, slots),
        cost_estimate=pl.CostEstimate(flops=0, transcendentals=0, bytes_accessed=4 * reach * width * 4),
        compiler_params=pltpu.CompilerParams(vmem_limit_bytes=6 << 20),
        name="edges",
    )(owners, *blocks)


def spread_kernel(count, slots, pieces, steps, owner_ref, power_ref, science_ref, *rest):
    blocks = rest[: len(steps)]
    out_ref, place, seen, held, sems = rest[-5:]
    me = lax.axis_index("visit")
    power = power_ref[0]
    find_places(count, slots, pieces, me, owner_ref, place, seen)
    for stage in range(2):
        for number, position, slot, k in each_slot(count, slots, me, place, steps):

            def go(number=number, position=position, slot=slot, k=k, stage=stage):
                store = pltpu.make_async_copy(held.at[number], out_ref.at[:, at_piece(k)], sems.at[number])
                if stage == 0:
                    held[number] = science_ref[:, at_piece(k)] + power * blocks[position][slot]
                    store.start()
                else:
                    store.wait()

            when_taken(count, slots, pieces, k, go)


def spread(owners, power, science_var, blocks, steps, count, partial=None):
    pieces = owners.shape[1]
    slots, rows = blocks[0].shape[:2]
    number = slots * len(steps)
    size = number * rows * PIECE
    before = [] if partial is None else [partial]
    return pl.pallas_call(
        functools.partial(spread_kernel, count, slots, pieces, steps),
        out_shape=jax.ShapeDtypeStruct(science_var.shape, jnp.float32),
        in_specs=[pl.BlockSpec(memory_space=SMEM)] * 2
        + [pl.BlockSpec(memory_space=VMEM)] * (1 + len(steps))
        + [pl.BlockSpec(memory_space=pl.ANY)] * len(before),
        out_specs=pl.BlockSpec(memory_space=pl.ANY),
        input_output_aliases={3 + len(steps): 0} if before else {},
        scratch_shapes=places_scratch(count, slots)
        + [pltpu.VMEM((number, rows, PIECE), jnp.float32), pltpu.SemaphoreType.DMA((number,))],
        cost_estimate=pl.CostEstimate(flops=2 * size, transcendentals=0, bytes_accessed=3 * size * 4),
        compiler_params=pltpu.CompilerParams(vmem_limit_bytes=6 << 20),
        name="spread",
    )(owners, power, science_var, *blocks, *before)


def split(x):
    high = x.astype(jnp.bfloat16)
    return high, (x - high.astype(jnp.float32)).astype(jnp.bfloat16)


def band_kernel(taps_ref, both_ref):
    deep = taps_ref.shape[1]
    half = both_ref.shape[0] // 2
    for q in range(GROUP):
        for at in range(0, deep, PIECE):
            line = jnp.broadcast_to(taps_ref[q : q + 1, at : at + PIECE], (SUB, PIECE))
            high, low = split(pltpu.roll(line, 0, 1, stride=1, stride_axis=0))
            both_ref[q * SUB : (q + 1) * SUB, at : at + PIECE] = high
            both_ref[half + q * SUB : half + (q + 1) * SUB, at : at + PIECE] = low


def bands(taps, window, lead):
    side = taps.shape[0]
    shifts = -(-side // GROUP)
    taps = jnp.pad(taps, ((0, shifts * GROUP - side), (lead, window - lead - side)))
    taps = taps.reshape(shifts, GROUP, window).transpose(1, 0, 2).reshape(GROUP, shifts * window)
    deep = -(-shifts * window // PIECE) * PIECE
    taps = jnp.pad(taps, ((0, 0), (0, deep - shifts * window)))
    return pl.pallas_call(
        band_kernel,
        out_shape=jax.ShapeDtypeStruct((2 * GROUP * SUB, deep), jnp.bfloat16),
        in_specs=[pl.BlockSpec(memory_space=VMEM)],
        out_specs=pl.BlockSpec(memory_space=VMEM),
        cost_estimate=pl.CostEstimate(flops=0, transcendentals=0, bytes_accessed=4 * GROUP * SUB * deep),
        compiler_params=pltpu.CompilerParams(vmem_limit_bytes=4 << 20),
        name="bands",
    )(taps)


def turn(x, lanes):
    return pltpu.roll(x, PIECE - lanes, 1)


def match_kernel(margin, shifts, count, slots, pieces, owner_ref, both_ref, above_ref, below_ref, science_ref, *rest):
    images, out_ref, rest = rest[:count], rest[count], rest[count + 1 :]
    place, seen, wide, high0, high1, low0, low1, part0, part1, kept_image, kept_part, result, sems = rest
    rows, width = science_ref.shape
    reach = above_ref.shape[0]
    window = SUB + 2 * reach
    filled = rows + 2 * reach
    half = both_ref.shape[0] // 2
    high, low, part = (high0, high1), (low0, low1), (part0, part1)
    me = lax.axis_index("visit")
    find_places(count, slots, pieces, me, owner_ref, place, seen)
    for _, position, slot, k in each_slot(count, slots, me, place, range(count)):

        def put(position=position, slot=slot, k=k):
            wide[reach : reach + rows, at_piece(k + 1)] = images[position][slot]

        when_taken(count, slots, pieces, k, put)
    wide[:, 0:PIECE] = jnp.zeros((filled, PIECE), jnp.float32)
    wide[:, PIECE + width :] = jnp.zeros((filled, wide.shape[1] - PIECE - width), jnp.float32)
    wide[0:reach, PIECE : PIECE + width] = above_ref[...]
    wide[reach + rows :, PIECE : PIECE + width] = below_ref[...]
    blocks = width // BLOCK
    lane_image = lax.broadcasted_iota(jnp.int32, (filled, PIECE), 1)
    lane_part = lax.broadcasted_iota(jnp.int32, (SUB, PIECE), 1)

    def store(b):
        columns = pl.ds(pl.multiple_of(b * BLOCK, BLOCK), BLOCK)
        return pltpu.make_async_copy(result.at[:, columns], out_ref.at[:, columns], sems.at[b])

    def build(b, parity, first=False):
        begin = b * BLOCK
        for m in range(shifts):
            offset = PIECE - margin + m * GROUP
            lanes = offset % PIECE
            at = begin + offset - lanes
            span = slice(m * filled, (m + 1) * filled)

            def column(k, at=at):
                return wide[:, pl.ds(pl.multiple_of(at + k * PIECE, PIECE), PIECE)]

            if lanes:
                turned = [turn(column(0), lanes) if first else kept_image[span, :]]
                turned += [turn(column(k), lanes) for k in (1, 2)]
                kept_image[span, :] = turned[2]
                mask = lane_image < PIECE - lanes
                parts = [jnp.where(mask, turned[k], turned[k + 1]) for k in (0, 1)]
            else:
                parts = [column(0), column(1)]
            for k in (0, 1):
                near, rest = split(parts[k])
                high[parity][span, k * PIECE : (k + 1) * PIECE] = near
                low[parity][span, k * PIECE : (k + 1) * PIECE] = rest

    def multiply(parity, columns=BLOCK):
        for top in range(0, rows, SUB):
            spans = [slice(m * filled + top, m * filled + top + window) for m in range(shifts)]
            near = jnp.concatenate([high[parity][span, :columns] for span in spans], axis=0)
            rest = jnp.concatenate([low[parity][span, :columns] for span in spans], axis=0)
            deep = near.shape[0]
            product = jnp.dot(both_ref[:half, :deep], rest, preferred_element_type=jnp.float32)
            pair = jnp.dot(both_ref[:, :deep], near, preferred_element_type=jnp.float32)
            part[parity][top * GROUP : (top + SUB) * GROUP, :columns] = product + (pair[:half] + pair[half:])

    def keep():
        for first in range(0, rows * GROUP, SUB):
            q = first // SUB % GROUP
            if q:
                kept_part[first : first + SUB, :] = turn(part0[first : first + SUB, :PIECE], q)

    def join(b, parity):
        here, after = part[parity], part[1 - parity]
        begin = pl.multiple_of(b * BLOCK, BLOCK)
        for top in range(0, rows, SUB):
            span = slice(top * GROUP, top * GROUP + SUB)
            totals = [here[span, :PIECE], here[span, PIECE:]]
            for q in range(1, GROUP):
                span = slice(top * GROUP + q * SUB, top * GROUP + (q + 1) * SUB)
                turned = [kept_part[span, :], turn(here[span, PIECE:], q), turn(after[span, :PIECE], q)]
                kept_part[span, :] = turned[2]
                for k in (0, 1):
                    totals[k] = totals[k] + jnp.where(lane_part < PIECE - q, turned[k], turned[k + 1])
            for k in (0, 1):
                at = pl.ds(pl.multiple_of(begin + k * PIECE, PIECE), PIECE)
                result[top : top + SUB, at] = science_ref[top : top + SUB, at] - totals[k]
        store(b).start()

    build(0, 0, first=True)
    build(1, 1)
    multiply(0)
    keep()
    build(2, 0)
    multiply(1)

    @pl.loop(1, blocks // 2)
    def _(p):
        b = p * 2
        join(b - 2, 0)
        build(b + 1, 1)
        multiply(0)
        join(b - 1, 1)
        build(b + 2, 0)
        multiply(1)

    join(blocks - 2, 0)
    multiply(0, PIECE)
    join(blocks - 1, 1)
    for b in range(blocks):
        store(b).wait()


def match(margin, shifts, owners, both, above, below, science, images):
    rows, width = science.shape
    count, pieces = len(images), owners.shape[1]
    slots = images[0].shape[0]
    reach = above.shape[0]
    filled = rows + 2 * reach
    return pl.pallas_call(
        functools.partial(match_kernel, margin, shifts, count, slots, pieces),
        out_shape=jax.ShapeDtypeStruct(science.shape, jnp.float32),
        in_specs=[pl.BlockSpec(memory_space=SMEM)]
        + [pl.BlockSpec(memory_space=VMEM)] * (4 + count),
        out_specs=pl.BlockSpec(memory_space=pl.ANY),
        scratch_shapes=places_scratch(count, slots)
        + [
            pltpu.VMEM((filled, width + BLOCK + 2 * PIECE), jnp.float32),
            *[pltpu.VMEM((shifts * filled, BLOCK), jnp.bfloat16)] * 4,
            *[pltpu.VMEM((GROUP * rows, BLOCK), jnp.float32)] * 2,
            pltpu.VMEM((shifts * filled, PIECE), jnp.float32),
            pltpu.VMEM((GROUP * rows, PIECE), jnp.float32),
            pltpu.VMEM((rows, width), jnp.float32),
            pltpu.SemaphoreType.DMA((width // BLOCK,)),
        ],
        cost_estimate=pl.CostEstimate(
            flops=6 * GROUP * rows * both.shape[1] * width, transcendentals=0, bytes_accessed=4 * rows * width * 4
        ),
        compiler_params=pltpu.CompilerParams(vmem_limit_bytes=20 << 20),
        name="match",
    )(owners, both, above, below, science, *images)


def local(
    science,
    science_var,
    template,
    template_var,
    intersection,
    col_offset,
    basis_row,
    basis_col,
    coef_sets,
    tile_coef,
):
    count = lax.axis_size("visit")
    pieces = intersection.shape[1]
    slots = max(2, pieces // count)
    _, width = science.shape[1:]
    side = basis_row.shape[1]
    margin = (side - 1) // 2
    reach = -(-margin // 8) * 8
    me = lax.axis_index("visit")
    tile_me = lax.axis_index("tile")
    highest = lax.Precision.HIGHEST
    owners = intersection[:, :, 0]
    mine = cut(owners, col_offset, template[0], count, slots)
    got = list(mine)
    for step in flux_steps(count):
        got[step] = lax.ppermute(mine[step], "visit", pairs(step, count))
    mine_var = cut(owners, col_offset, template_var[0], count, slots)
    got_var = list(mine_var)
    for step in near_steps(count) + far_steps(count):
        got_var[step] = lax.ppermute(mine_var[step], "visit", pairs(step, count))

    chosen = lax.dynamic_slice(tile_coef, (me, tile_me), (1, 1))[0, 0]
    coeffs = lax.dynamic_index_in_dim(coef_sets, chosen, 0, keepdims=False)
    taps = jnp.einsum("bc,ba->ca", coeffs[:, None] * basis_col, basis_row, precision=highest)
    power = jnp.sum(taps * taps).reshape(1)
    both = bands(taps, SUB + 2 * reach, reach - margin)

    head, tail = edges(owners, got, width, reach)
    tiles = lax.axis_size("tile")
    above = lax.ppermute(tail, "tile", [(i, i + 1) for i in range(tiles - 1)])
    below = lax.ppermute(head, "tile", [(i + 1, i) for i in range(tiles - 1)])
    first = [0] + near_steps(count)
    blocks = [got_var[step] for step in first]
    difference_var = spread(owners, power, science_var[0], blocks, first, count)
    shifts = -(-side // GROUP)
    difference = match(margin, shifts, owners, both, above, below, science[0], got)
    second = far_steps(count)
    blocks = [got_var[step] for step in second]
    difference_var = spread(owners, power, science_var[0], blocks, second, count, difference_var)
    return difference[None], difference_var[None]


def near_steps(count):
    return list(range(1, count // 2))


def far_steps(count):
    return list(range(count // 2, count))


def flux_steps(count):
    far = far_steps(count)
    return far[-1:] + near_steps(count) + far[1:-1] + far[:1]


def solution(mesh):
    split_spec = P("visit", "tile", None)
    return jax.shard_map(
        local,
        mesh=mesh,
        in_specs=(split_spec,) * 4 + (P(),) * 6,
        out_specs=(split_spec, split_spec),
        check_vma=False,
    )
```

```python
import functools

import jax
import jax.numpy as jnp
from jax import lax
from jax.experimental import pallas as pl
from jax.experimental.pallas import tpu as pltpu
from jax.sharding import PartitionSpec as P


PIECE = 128
GROUP = 11
SUB = 16
BLOCK = 256


SMEM = pltpu.MemorySpace.SMEM
VMEM = pltpu.MemorySpace.VMEM
HBM = pltpu.MemorySpace.HBM


def partner(me, step, count):
    if count & (count - 1) == 0:
        return me ^ step
    return lax.rem(me + step, count)


def sender(me, step, count):
    if count & (count - 1) == 0:
        return me ^ step
    return lax.rem(me + count - step, count)


def pairs(step, count):
    if count & (count - 1) == 0:
        return [(i, i ^ step) for i in range(count)]
    return [(i, (i + step) % count) for i in range(count)]


def cut_kernel(count, slots, pieces, owner_hbm, offset_hbm, strip_hbm, *rest):
    outs, (strip, owner_ref, offset_ref, starts, sems) = rest[:count], rest[count:]
    me = lax.axis_index("visit")
    rows, width = strip.shape
    last = width // PIECE - 1
    loads = [
        pltpu.make_async_copy(source, target, sems.at[i])
        for i, (source, target) in enumerate(((owner_hbm, owner_ref), (offset_hbm, offset_ref), (strip_hbm, strip)))
    ]
    for load in loads:
        load.start()
    for load in loads[:2]:
        load.wait()
    for step in range(count):
        visit = partner(me, step, count)
        begin = step * (slots + 1)
        for slot in range(slots):
            starts[begin + slot] = 0
        found = jnp.int32(begin)
        for k in range(pieces):
            starts[found] = offset_ref[visit, k]
            found = found + (owner_ref[visit, k] == me).astype(jnp.int32)
    loads[2].wait()
    lane = lax.broadcasted_iota(jnp.int32, (rows, PIECE), 1)
    for step in range(count):
        for slot in range(slots):
            start = starts[step * (slots + 1) + slot]
            block = start // PIECE
            shift = lax.rem(start, PIECE)
            after = jnp.minimum(block + 1, last)
            left = strip[:, pl.ds(pl.multiple_of(block * PIECE, PIECE), PIECE)]
            right = strip[:, pl.ds(pl.multiple_of(after * PIECE, PIECE), PIECE)]
            joined = jnp.where(lane < shift, right, left)
            outs[step][slot] = pltpu.roll(joined, lax.rem(PIECE - shift, PIECE), 1)


def cut(owners, offsets, strip, count, slots):
    rows, width = strip.shape
    shape = jax.ShapeDtypeStruct((slots, rows, PIECE), jnp.float32)
    return pl.pallas_call(
        functools.partial(cut_kernel, count, slots, owners.shape[1]),
        out_shape=[shape] * count,
        in_specs=[pl.BlockSpec(memory_space=HBM)] * 3,
        out_specs=[pl.BlockSpec(memory_space=VMEM)] * count,
        scratch_shapes=[
            pltpu.VMEM((rows, width), jnp.float32),
            pltpu.SMEM(owners.shape, jnp.int32),
            pltpu.SMEM(offsets.shape, jnp.int32),
            pltpu.SMEM((count * (slots + 1),), jnp.int32),
            pltpu.SemaphoreType.DMA((3,)),
        ],
        cost_estimate=pl.CostEstimate(flops=0, transcendentals=0, bytes_accessed=2 * strip.size * 4),
        name="cut",
    )(owners, offsets, strip)


def find_places(count, slots, pieces, me, owner_ref, place, seen):
    for owner in range(count):
        seen[owner] = 0
    for entry in range(count * slots):
        place[entry] = -1

    def find(k, carry):
        owner = owner_ref[me, k]
        nth = seen[owner]
        place[owner * slots + nth] = k
        seen[owner] = nth + 1
        return carry

    lax.fori_loop(0, pieces, find, jnp.int32(0), unroll=8)


def when_taken(count, slots, pieces, k, body):
    if count * slots == pieces:
        body()
    else:
        pl.when(k >= 0)(body)


def at_piece(k):
    return pl.ds(pl.multiple_of(k * PIECE, PIECE), PIECE)


def each_slot(count, slots, me, place, steps):
    number = 0
    for position, step in enumerate(steps):
        owner = sender(me, step, count)
        for slot in range(slots):
            yield number, position, slot, place[owner * slots + slot]
            number += 1


def places_scratch(count, slots):
    return [pltpu.SMEM((count * slots,), jnp.int32), pltpu.SMEM((count,), jnp.int32)]


def edges_kernel(count, slots, pieces, reach, owner_ref, *rest):
    blocks = rest[:count]
    head_ref, tail_ref, place, seen = rest[count:]
    me = lax.axis_index("visit")
    rows = blocks[0].shape[1]
    find_places(count, slots, pieces, me, owner_ref, place, seen)
    for _, position, slot, k in each_slot(count, slots, me, place, range(count)):

        def put(position=position, slot=slot, k=k):
            head_ref[:, at_piece(k)] = blocks[position][slot, :reach]
            tail_ref[:, at_piece(k)] = blocks[position][slot, rows - reach :]

        when_taken(count, slots, pieces, k, put)


def edges(owners, blocks, width, reach):
    count, pieces = len(blocks), owners.shape[1]
    slots = blocks[0].shape[0]
    shape = jax.ShapeDtypeStruct((reach, width), jnp.float32)
    return pl.pallas_call(
        functools.partial(edges_kernel, count, slots, pieces, reach),
        out_shape=[shape, shape],
        in_specs=[pl.BlockSpec(memory_space=SMEM)] + [pl.BlockSpec(memory_space=VMEM)] * count,
        out_specs=[pl.BlockSpec(memory_space=VMEM)] * 2,
        scratch_shapes=places_scratch(count, slots),
        cost_estimate=pl.CostEstimate(flops=0, transcendentals=0, bytes_accessed=4 * reach * width * 4),
        compiler_params=pltpu.CompilerParams(vmem_limit_bytes=6 << 20),
        name="edges",
    )(owners, *blocks)


def early_kernel(count, slots, pieces, steps, owner_ref, power_ref, science_ref, *rest):
    blocks = rest[: len(steps)]
    out_ref, place, seen = rest[len(steps) :]
    me = lax.axis_index("visit")
    power = power_ref[0]
    find_places(count, slots, pieces, me, owner_ref, place, seen)
    for _, position, slot, k in each_slot(count, slots, me, place, steps):

        def put(position=position, slot=slot, k=k):
            out_ref[:, at_piece(k)] = science_ref[:, at_piece(k)] + power * blocks[position][slot]

        when_taken(count, slots, pieces, k, put)


def early_spread(owners, power, science_var, blocks, steps, count):
    pieces = owners.shape[1]
    slots, rows = blocks[0].shape[:2]
    size = slots * len(steps) * rows * PIECE
    return pl.pallas_call(
        functools.partial(early_kernel, count, slots, pieces, steps),
        out_shape=jax.ShapeDtypeStruct(science_var.shape, jnp.float32),
        in_specs=[pl.BlockSpec(memory_space=SMEM)] * 2 + [pl.BlockSpec(memory_space=VMEM)] * (1 + len(steps)),
        out_specs=pl.BlockSpec(memory_space=VMEM),
        scratch_shapes=places_scratch(count, slots),
        cost_estimate=pl.CostEstimate(flops=2 * size, transcendentals=0, bytes_accessed=3 * size * 4),
        compiler_params=pltpu.CompilerParams(vmem_limit_bytes=6 << 20),
        name="early",
    )(owners, power, science_var, *blocks)


def late_kernel(count, slots, pieces, first, steps, owner_ref, power_ref, science_ref, early_ref, *rest):
    blocks = rest[: len(steps)]
    out_ref, place, seen, held, early_sems, sems = rest[len(steps) :]
    me = lax.axis_index("visit")
    power = power_ref[0]
    find_places(count, slots, pieces, me, owner_ref, place, seen)

    def store_early(number, k):
        return pltpu.make_async_copy(early_ref.at[:, at_piece(k)], out_ref.at[:, at_piece(k)], early_sems.at[number])

    def store_late(number, k):
        return pltpu.make_async_copy(held.at[number], out_ref.at[:, at_piece(k)], sems.at[number])

    for number, _, _, k in each_slot(count, slots, me, place, first):
        when_taken(count, slots, pieces, k, lambda number=number, k=k: store_early(number, k).start())
    for number, position, slot, k in each_slot(count, slots, me, place, steps):

        def put(number=number, position=position, slot=slot, k=k):
            held[number] = science_ref[:, at_piece(k)] + power * blocks[position][slot]
            store_late(number, k).start()

        when_taken(count, slots, pieces, k, put)
    for number, _, _, k in each_slot(count, slots, me, place, first):
        when_taken(count, slots, pieces, k, lambda number=number, k=k: store_early(number, k).wait())
    for number, _, _, k in each_slot(count, slots, me, place, steps):
        when_taken(count, slots, pieces, k, lambda number=number, k=k: store_late(number, k).wait())


def late_spread(owners, power, science_var, early, blocks, first, steps, count):
    pieces = owners.shape[1]
    slots, rows = blocks[0].shape[:2]
    number = slots * len(steps)
    size = number * rows * PIECE
    return pl.pallas_call(
        functools.partial(late_kernel, count, slots, pieces, first, steps),
        out_shape=jax.ShapeDtypeStruct(science_var.shape, jnp.float32),
        in_specs=[pl.BlockSpec(memory_space=SMEM)] * 2 + [pl.BlockSpec(memory_space=VMEM)] * (2 + len(steps)),
        out_specs=pl.BlockSpec(memory_space=pl.ANY),
        scratch_shapes=places_scratch(count, slots)
        + [
            pltpu.VMEM((number, rows, PIECE), jnp.float32),
            pltpu.SemaphoreType.DMA((slots * len(first),)),
            pltpu.SemaphoreType.DMA((number,)),
        ],
        cost_estimate=pl.CostEstimate(flops=2 * size, transcendentals=0, bytes_accessed=4 * size * 4),
        compiler_params=pltpu.CompilerParams(vmem_limit_bytes=6 << 20),
        name="late",
    )(owners, power, science_var, early, *blocks)


def split(x):
    high = x.astype(jnp.bfloat16)
    return high, (x - high.astype(jnp.float32)).astype(jnp.bfloat16)


def band_kernel(taps_ref, both_ref):
    deep = taps_ref.shape[1]
    half = both_ref.shape[0] // 2
    for q in range(GROUP):
        for at in range(0, deep, PIECE):
            line = jnp.broadcast_to(taps_ref[q : q + 1, at : at + PIECE], (SUB, PIECE))
            high, low = split(pltpu.roll(line, 0, 1, stride=1, stride_axis=0))
            both_ref[q * SUB : (q + 1) * SUB, at : at + PIECE] = high
            both_ref[half + q * SUB : half + (q + 1) * SUB, at : at + PIECE] = low


def bands(taps, window, lead):
    side = taps.shape[0]
    shifts = -(-side // GROUP)
    taps = jnp.pad(taps, ((0, shifts * GROUP - side), (lead, window - lead - side)))
    taps = taps.reshape(shifts, GROUP, window).transpose(1, 0, 2).reshape(GROUP, shifts * window)
    deep = -(-shifts * window // PIECE) * PIECE
    taps = jnp.pad(taps, ((0, 0), (0, deep - shifts * window)))
    return pl.pallas_call(
        band_kernel,
        out_shape=jax.ShapeDtypeStruct((2 * GROUP * SUB, deep), jnp.bfloat16),
        in_specs=[pl.BlockSpec(memory_space=VMEM)],
        out_specs=pl.BlockSpec(memory_space=VMEM),
        cost_estimate=pl.CostEstimate(flops=0, transcendentals=0, bytes_accessed=4 * GROUP * SUB * deep),
        compiler_params=pltpu.CompilerParams(vmem_limit_bytes=4 << 20),
        name="bands",
    )(taps)


def turn(x, lanes):
    return pltpu.roll(x, PIECE - lanes, 1)


def match_kernel(margin, shifts, count, slots, pieces, owner_ref, both_ref, above_ref, below_ref, science_ref, *rest):
    images, out_ref, rest = rest[:count], rest[count], rest[count + 1 :]
    place, seen, wide, high0, high1, low0, low1, part0, part1, kept_image, kept_part, result, sems = rest
    rows, width = science_ref.shape
    reach = above_ref.shape[0]
    window = SUB + 2 * reach
    filled = rows + 2 * reach
    half = both_ref.shape[0] // 2
    high, low, part = (high0, high1), (low0, low1), (part0, part1)
    me = lax.axis_index("visit")
    find_places(count, slots, pieces, me, owner_ref, place, seen)
    for _, position, slot, k in each_slot(count, slots, me, place, range(count)):

        def put(position=position, slot=slot, k=k):
            wide[reach : reach + rows, at_piece(k + 1)] = images[position][slot]

        when_taken(count, slots, pieces, k, put)
    wide[:, 0:PIECE] = jnp.zeros((filled, PIECE), jnp.float32)
    wide[:, PIECE + width :] = jnp.zeros((filled, wide.shape[1] - PIECE - width), jnp.float32)
    wide[0:reach, PIECE : PIECE + width] = above_ref[...]
    wide[reach + rows :, PIECE : PIECE + width] = below_ref[...]
    blocks = width // BLOCK
    lane_image = lax.broadcasted_iota(jnp.int32, (filled, PIECE), 1)
    lane_part = lax.broadcasted_iota(jnp.int32, (SUB, PIECE), 1)

    def store(b):
        columns = pl.ds(pl.multiple_of(b * BLOCK, BLOCK), BLOCK)
        return pltpu.make_async_copy(result.at[:, columns], out_ref.at[:, columns], sems.at[b])

    def build(b, parity, first=False):
        begin = b * BLOCK
        for m in range(shifts):
            offset = PIECE - margin + m * GROUP
            lanes = offset % PIECE
            at = begin + offset - lanes
            span = slice(m * filled, (m + 1) * filled)

            def column(k, at=at):
                return wide[:, pl.ds(pl.multiple_of(at + k * PIECE, PIECE), PIECE)]

            if lanes:
                turned = [turn(column(0), lanes) if first else kept_image[span, :]]
                turned += [turn(column(k), lanes) for k in (1, 2)]
                kept_image[span, :] = turned[2]
                mask = lane_image < PIECE - lanes
                parts = [jnp.where(mask, turned[k], turned[k + 1]) for k in (0, 1)]
            else:
                parts = [column(0), column(1)]
            for k in (0, 1):
                near, rest = split(parts[k])
                high[parity][span, k * PIECE : (k + 1) * PIECE] = near
                low[parity][span, k * PIECE : (k + 1) * PIECE] = rest

    def multiply(parity, columns=BLOCK):
        for top in range(0, rows, SUB):
            spans = [slice(m * filled + top, m * filled + top + window) for m in range(shifts)]
            near = jnp.concatenate([high[parity][span, :columns] for span in spans], axis=0)
            rest = jnp.concatenate([low[parity][span, :columns] for span in spans], axis=0)
            deep = near.shape[0]
            product = jnp.dot(both_ref[:half, :deep], rest, preferred_element_type=jnp.float32)
            pair = jnp.dot(both_ref[:, :deep], near, preferred_element_type=jnp.float32)
            part[parity][top * GROUP : (top + SUB) * GROUP, :columns] = product + (pair[:half] + pair[half:])

    def keep():
        for first in range(0, rows * GROUP, SUB):
            q = first // SUB % GROUP
            if q:
                kept_part[first : first + SUB, :] = turn(part0[first : first + SUB, :PIECE], q)

    def join(b, parity):
        here, after = part[parity], part[1 - parity]
        begin = pl.multiple_of(b * BLOCK, BLOCK)
        for top in range(0, rows, SUB):
            span = slice(top * GROUP, top * GROUP + SUB)
            totals = [here[span, :PIECE], here[span, PIECE:]]
            for q in range(1, GROUP):
                span = slice(top * GROUP + q * SUB, top * GROUP + (q + 1) * SUB)
                turned = [kept_part[span, :], turn(here[span, PIECE:], q), turn(after[span, :PIECE], q)]
                kept_part[span, :] = turned[2]
                for k in (0, 1):
                    totals[k] = totals[k] + jnp.where(lane_part < PIECE - q, turned[k], turned[k + 1])
            for k in (0, 1):
                at = pl.ds(pl.multiple_of(begin + k * PIECE, PIECE), PIECE)
                result[top : top + SUB, at] = science_ref[top : top + SUB, at] - totals[k]
        store(b).start()

    build(0, 0, first=True)
    build(1, 1)
    multiply(0)
    keep()
    build(2, 0)
    multiply(1)

    @pl.loop(1, blocks // 2)
    def _(p):
        b = p * 2
        join(b - 2, 0)
        build(b + 1, 1)
        multiply(0)
        join(b - 1, 1)
        build(b + 2, 0)
        multiply(1)

    join(blocks - 2, 0)
    multiply(0, PIECE)
    join(blocks - 1, 1)
    for b in range(blocks):
        store(b).wait()


def match(margin, shifts, owners, both, above, below, science, images):
    rows, width = science.shape
    count, pieces = len(images), owners.shape[1]
    slots = images[0].shape[0]
    reach = above.shape[0]
    filled = rows + 2 * reach
    return pl.pallas_call(
        functools.partial(match_kernel, margin, shifts, count, slots, pieces),
        out_shape=jax.ShapeDtypeStruct(science.shape, jnp.float32),
        in_specs=[pl.BlockSpec(memory_space=SMEM)]
        + [pl.BlockSpec(memory_space=VMEM)] * (4 + count),
        out_specs=pl.BlockSpec(memory_space=pl.ANY),
        scratch_shapes=places_scratch(count, slots)
        + [
            pltpu.VMEM((filled, width + BLOCK + 2 * PIECE), jnp.float32),
            *[pltpu.VMEM((shifts * filled, BLOCK), jnp.bfloat16)] * 4,
            *[pltpu.VMEM((GROUP * rows, BLOCK), jnp.float32)] * 2,
            pltpu.VMEM((shifts * filled, PIECE), jnp.float32),
            pltpu.VMEM((GROUP * rows, PIECE), jnp.float32),
            pltpu.VMEM((rows, width), jnp.float32),
            pltpu.SemaphoreType.DMA((width // BLOCK,)),
        ],
        cost_estimate=pl.CostEstimate(
            flops=6 * GROUP * rows * both.shape[1] * width, transcendentals=0, bytes_accessed=4 * rows * width * 4
        ),
        compiler_params=pltpu.CompilerParams(vmem_limit_bytes=20 << 20),
        name="match",
    )(owners, both, above, below, science, *images)


def local(
    science,
    science_var,
    template,
    template_var,
    intersection,
    col_offset,
    basis_row,
    basis_col,
    coef_sets,
    tile_coef,
):
    count = lax.axis_size("visit")
    pieces = intersection.shape[1]
    slots = max(2, pieces // count)
    _, width = science.shape[1:]
    side = basis_row.shape[1]
    margin = (side - 1) // 2
    reach = -(-margin // 8) * 8
    me = lax.axis_index("visit")
    tile_me = lax.axis_index("tile")
    highest = lax.Precision.HIGHEST
    owners = intersection[:, :, 0]
    mine = cut(owners, col_offset, template[0], count, slots)
    got = list(mine)
    for step in flux_steps(count):
        got[step] = lax.ppermute(mine[step], "visit", pairs(step, count))
    mine_var = cut(owners, col_offset, template_var[0], count, slots)
    got_var = list(mine_var)
    for step in near_steps(count) + far_steps(count):
        got_var[step] = lax.ppermute(mine_var[step], "visit", pairs(step, count))

    chosen = lax.dynamic_slice(tile_coef, (me, tile_me), (1, 1))[0, 0]
    coeffs = lax.dynamic_index_in_dim(coef_sets, chosen, 0, keepdims=False)
    taps = jnp.einsum("bc,ba->ca", coeffs[:, None] * basis_col, basis_row, precision=highest)
    power = jnp.sum(taps * taps).reshape(1)
    both = bands(taps, SUB + 2 * reach, reach - margin)

    head, tail = edges(owners, got, width, reach)
    tiles = lax.axis_size("tile")
    above = lax.ppermute(tail, "tile", [(i, i + 1) for i in range(tiles - 1)])
    below = lax.ppermute(head, "tile", [(i + 1, i) for i in range(tiles - 1)])
    first, second = [0] + near_steps(count), far_steps(count)
    blocks = [got_var[step] for step in first]
    early = early_spread(owners, power, science_var[0], blocks, first, count)
    shifts = -(-side // GROUP)
    difference = match(margin, shifts, owners, both, above, below, science[0], got)
    blocks = [got_var[step] for step in second]
    difference_var = late_spread(owners, power, science_var[0], early, blocks, first, second, count)
    return difference[None], difference_var[None]


def near_steps(count):
    return list(range(1, count // 2))


def far_steps(count):
    return list(range(count // 2, count))


def flux_steps(count):
    far = far_steps(count)
    return near_steps(count) + far


def solution(mesh):
    split_spec = P("visit", "tile", None)
    return jax.shard_map(
        local,
        mesh=mesh,
        in_specs=(split_spec,) * 4 + (P(),) * 6,
        out_specs=(split_spec, split_spec),
        check_vma=False,
    )
```

```python
import functools

import jax
import jax.numpy as jnp
from jax import lax
from jax.experimental import pallas as pl
from jax.experimental.pallas import tpu as pltpu
from jax.sharding import PartitionSpec as P


PIECE = 128
GROUP = 11
SUB = 16
BLOCK = 256


SMEM = pltpu.MemorySpace.SMEM
VMEM = pltpu.MemorySpace.VMEM
HBM = pltpu.MemorySpace.HBM


def partner(me, step, count):
    if count & (count - 1) == 0:
        return me ^ step
    return lax.rem(me + step, count)


def sender(me, step, count):
    if count & (count - 1) == 0:
        return me ^ step
    return lax.rem(me + count - step, count)


def pairs(step, count):
    if count & (count - 1) == 0:
        return [(i, i ^ step) for i in range(count)]
    return [(i, (i + step) % count) for i in range(count)]


def cut_kernel(count, slots, pieces, owner_hbm, offset_hbm, strip_hbm, *rest):
    outs, (strip, owner_ref, offset_ref, starts, sems) = rest[:count], rest[count:]
    me = lax.axis_index("visit")
    rows, width = strip.shape
    last = width // PIECE - 1
    loads = [
        pltpu.make_async_copy(source, target, sems.at[i])
        for i, (source, target) in enumerate(((owner_hbm, owner_ref), (offset_hbm, offset_ref), (strip_hbm, strip)))
    ]
    for load in loads:
        load.start()
    for load in loads[:2]:
        load.wait()
    for step in range(count):
        visit = partner(me, step, count)
        begin = step * (slots + 1)
        for slot in range(slots):
            starts[begin + slot] = 0
        found = jnp.int32(begin)
        for k in range(pieces):
            starts[found] = offset_ref[visit, k]
            found = found + (owner_ref[visit, k] == me).astype(jnp.int32)
    loads[2].wait()
    lane = lax.broadcasted_iota(jnp.int32, (rows, PIECE), 1)
    for step in range(count):
        for slot in range(slots):
            start = starts[step * (slots + 1) + slot]
            block = start // PIECE
            shift = lax.rem(start, PIECE)
            after = jnp.minimum(block + 1, last)
            left = strip[:, pl.ds(pl.multiple_of(block * PIECE, PIECE), PIECE)]
            right = strip[:, pl.ds(pl.multiple_of(after * PIECE, PIECE), PIECE)]
            joined = jnp.where(lane < shift, right, left)
            outs[step][slot] = pltpu.roll(joined, lax.rem(PIECE - shift, PIECE), 1)


def cut(owners, offsets, strip, count, slots):
    rows, width = strip.shape
    shape = jax.ShapeDtypeStruct((slots, rows, PIECE), jnp.float32)
    return pl.pallas_call(
        functools.partial(cut_kernel, count, slots, owners.shape[1]),
        out_shape=[shape] * count,
        in_specs=[pl.BlockSpec(memory_space=HBM)] * 3,
        out_specs=[pl.BlockSpec(memory_space=VMEM)] * count,
        scratch_shapes=[
            pltpu.VMEM((rows, width), jnp.float32),
            pltpu.SMEM(owners.shape, jnp.int32),
            pltpu.SMEM(offsets.shape, jnp.int32),
            pltpu.SMEM((count * (slots + 1),), jnp.int32),
            pltpu.SemaphoreType.DMA((3,)),
        ],
        cost_estimate=pl.CostEstimate(flops=0, transcendentals=0, bytes_accessed=2 * strip.size * 4),
        name="cut",
    )(owners, offsets, strip)


def find_places(count, slots, pieces, me, owner_ref, place, seen):
    for owner in range(count):
        seen[owner] = 0
    for entry in range(count * slots):
        place[entry] = -1

    def find(k, carry):
        owner = owner_ref[me, k]
        nth = seen[owner]
        place[owner * slots + nth] = k
        seen[owner] = nth + 1
        return carry

    lax.fori_loop(0, pieces, find, jnp.int32(0), unroll=8)


def when_taken(count, slots, pieces, k, body):
    if count * slots == pieces:
        body()
    else:
        pl.when(k >= 0)(body)


def at_piece(k):
    return pl.ds(pl.multiple_of(k * PIECE, PIECE), PIECE)


def each_slot(count, slots, me, place, steps):
    number = 0
    for position, step in enumerate(steps):
        owner = sender(me, step, count)
        for slot in range(slots):
            yield number, position, slot, place[owner * slots + slot]
            number += 1


def edges_kernel(count, slots, pieces, reach, place, *rest):
    blocks = rest[:count]
    head_ref, tail_ref = rest[count:]
    me = lax.axis_index("visit")
    rows = blocks[0].shape[1]
    for _, position, slot, k in each_slot(count, slots, me, place, range(count)):

        def put(position=position, slot=slot, k=k):
            head_ref[:, at_piece(k)] = blocks[position][slot, :reach]
            tail_ref[:, at_piece(k)] = blocks[position][slot, rows - reach :]

        when_taken(count, slots, pieces, k, put)


def edges(places, pieces, blocks, width, reach):
    count = len(blocks)
    slots = blocks[0].shape[0]
    shape = jax.ShapeDtypeStruct((reach, width), jnp.float32)
    return pl.pallas_call(
        functools.partial(edges_kernel, count, slots, pieces, reach),
        out_shape=[shape, shape],
        in_specs=[pl.BlockSpec(memory_space=SMEM)] + [pl.BlockSpec(memory_space=VMEM)] * count,
        out_specs=[pl.BlockSpec(memory_space=VMEM)] * 2,
        cost_estimate=pl.CostEstimate(flops=0, transcendentals=0, bytes_accessed=4 * reach * width * 4),
        compiler_params=pltpu.CompilerParams(vmem_limit_bytes=6 << 20),
        name="edges",
    )(places, *blocks)


def early_kernel(count, slots, pieces, steps, place, power_ref, science_ref, *rest):
    blocks = rest[: len(steps)]
    (out_ref,) = rest[len(steps) :]
    me = lax.axis_index("visit")
    power = power_ref[0]
    for _, position, slot, k in each_slot(count, slots, me, place, steps):

        def put(position=position, slot=slot, k=k):
            out_ref[:, at_piece(k)] = science_ref[:, at_piece(k)] + power * blocks[position][slot]

        when_taken(count, slots, pieces, k, put)


def early_spread(places, pieces, power, science_var, blocks, steps, count):
    slots, rows = blocks[0].shape[:2]
    size = slots * len(steps) * rows * PIECE
    return pl.pallas_call(
        functools.partial(early_kernel, count, slots, pieces, steps),
        out_shape=jax.ShapeDtypeStruct(science_var.shape, jnp.float32),
        in_specs=[pl.BlockSpec(memory_space=SMEM)] * 2 + [pl.BlockSpec(memory_space=VMEM)] * (1 + len(steps)),
        out_specs=pl.BlockSpec(memory_space=VMEM),
        cost_estimate=pl.CostEstimate(flops=2 * size, transcendentals=0, bytes_accessed=3 * size * 4),
        compiler_params=pltpu.CompilerParams(vmem_limit_bytes=6 << 20),
        name="early",
    )(places, power, science_var, *blocks)


def late_kernel(count, slots, pieces, first, steps, place, power_ref, science_ref, early_ref, *rest):
    blocks = rest[: len(steps)]
    out_ref, held, early_sems, sems = rest[len(steps) :]
    me = lax.axis_index("visit")
    power = power_ref[0]

    def store_early(number, k):
        return pltpu.make_async_copy(early_ref.at[:, at_piece(k)], out_ref.at[:, at_piece(k)], early_sems.at[number])

    def store_late(number, k):
        return pltpu.make_async_copy(held.at[number], out_ref.at[:, at_piece(k)], sems.at[number])

    for number, _, _, k in each_slot(count, slots, me, place, first):
        when_taken(count, slots, pieces, k, lambda number=number, k=k: store_early(number, k).start())
    for number, position, slot, k in each_slot(count, slots, me, place, steps):

        def put(number=number, position=position, slot=slot, k=k):
            held[number] = science_ref[:, at_piece(k)] + power * blocks[position][slot]
            store_late(number, k).start()

        when_taken(count, slots, pieces, k, put)
    for number, _, _, k in each_slot(count, slots, me, place, first):
        when_taken(count, slots, pieces, k, lambda number=number, k=k: store_early(number, k).wait())
    for number, _, _, k in each_slot(count, slots, me, place, steps):
        when_taken(count, slots, pieces, k, lambda number=number, k=k: store_late(number, k).wait())


def late_spread(places, pieces, power, science_var, early, blocks, first, steps, count):
    slots, rows = blocks[0].shape[:2]
    number = slots * len(steps)
    size = number * rows * PIECE
    return pl.pallas_call(
        functools.partial(late_kernel, count, slots, pieces, first, steps),
        out_shape=jax.ShapeDtypeStruct(science_var.shape, jnp.float32),
        in_specs=[pl.BlockSpec(memory_space=SMEM)] * 2 + [pl.BlockSpec(memory_space=VMEM)] * (2 + len(steps)),
        out_specs=pl.BlockSpec(memory_space=pl.ANY),
        scratch_shapes=[
            pltpu.VMEM((number, rows, PIECE), jnp.float32),
            pltpu.SemaphoreType.DMA((slots * len(first),)),
            pltpu.SemaphoreType.DMA((number,)),
        ],
        cost_estimate=pl.CostEstimate(flops=2 * size, transcendentals=0, bytes_accessed=4 * size * 4),
        compiler_params=pltpu.CompilerParams(vmem_limit_bytes=6 << 20),
        name="late",
    )(places, power, science_var, early, *blocks)


def split(x):
    high = x.astype(jnp.bfloat16)
    return high, (x - high.astype(jnp.float32)).astype(jnp.bfloat16)


def band_kernel(count, slots, taps_ref, owner_ref, both_ref, place, seen):
    find_places(count, slots, owner_ref.shape[1], lax.axis_index("visit"), owner_ref, place, seen)
    deep = taps_ref.shape[1]
    half = both_ref.shape[0] // 2
    for q in range(GROUP):
        for at in range(0, deep, PIECE):
            line = jnp.broadcast_to(taps_ref[q : q + 1, at : at + PIECE], (SUB, PIECE))
            high, low = split(pltpu.roll(line, 0, 1, stride=1, stride_axis=0))
            both_ref[q * SUB : (q + 1) * SUB, at : at + PIECE] = high
            both_ref[half + q * SUB : half + (q + 1) * SUB, at : at + PIECE] = low


def bands(taps, window, lead, owners, count, slots):
    side = taps.shape[0]
    shifts = -(-side // GROUP)
    taps = jnp.pad(taps, ((0, shifts * GROUP - side), (lead, window - lead - side)))
    taps = taps.reshape(shifts, GROUP, window).transpose(1, 0, 2).reshape(GROUP, shifts * window)
    deep = -(-shifts * window // PIECE) * PIECE
    taps = jnp.pad(taps, ((0, 0), (0, deep - shifts * window)))
    return pl.pallas_call(
        functools.partial(band_kernel, count, slots),
        out_shape=[
            jax.ShapeDtypeStruct((2 * GROUP * SUB, deep), jnp.bfloat16),
            jax.ShapeDtypeStruct((count * slots,), jnp.int32),
        ],
        in_specs=[pl.BlockSpec(memory_space=VMEM), pl.BlockSpec(memory_space=SMEM)],
        out_specs=[pl.BlockSpec(memory_space=VMEM), pl.BlockSpec(memory_space=SMEM)],
        scratch_shapes=[pltpu.SMEM((count,), jnp.int32)],
        cost_estimate=pl.CostEstimate(flops=0, transcendentals=0, bytes_accessed=4 * GROUP * SUB * deep),
        compiler_params=pltpu.CompilerParams(vmem_limit_bytes=4 << 20),
        name="bands",
    )(taps, owners)


def turn(x, lanes):
    return pltpu.roll(x, PIECE - lanes, 1)


def match_kernel(margin, shifts, count, slots, pieces, place, both_ref, above_ref, below_ref, science_ref, *rest):
    images, out_ref, rest = rest[:count], rest[count], rest[count + 1 :]
    wide, high0, high1, low0, low1, part0, part1, kept_image, kept_part, result, sems = rest
    rows, width = science_ref.shape
    reach = above_ref.shape[0]
    window = SUB + 2 * reach
    filled = rows + 2 * reach
    half = both_ref.shape[0] // 2
    high, low, part = (high0, high1), (low0, low1), (part0, part1)
    me = lax.axis_index("visit")
    for _, position, slot, k in each_slot(count, slots, me, place, range(count)):

        def put(position=position, slot=slot, k=k):
            wide[reach : reach + rows, at_piece(k + 1)] = images[position][slot]

        when_taken(count, slots, pieces, k, put)
    wide[:, 0:PIECE] = jnp.zeros((filled, PIECE), jnp.float32)
    wide[:, PIECE + width :] = jnp.zeros((filled, wide.shape[1] - PIECE - width), jnp.float32)
    wide[0:reach, PIECE : PIECE + width] = above_ref[...]
    wide[reach + rows :, PIECE : PIECE + width] = below_ref[...]
    blocks = width // BLOCK
    lane_image = lax.broadcasted_iota(jnp.int32, (filled, PIECE), 1)
    lane_part = lax.broadcasted_iota(jnp.int32, (SUB, PIECE), 1)

    def store(b):
        columns = pl.ds(pl.multiple_of(b * BLOCK, BLOCK), BLOCK)
        return pltpu.make_async_copy(result.at[:, columns], out_ref.at[:, columns], sems.at[b])

    def build(b, parity, first=False):
        begin = b * BLOCK
        for m in range(shifts):
            offset = PIECE - margin + m * GROUP
            lanes = offset % PIECE
            at = begin + offset - lanes
            span = slice(m * filled, (m + 1) * filled)

            def column(k, at=at):
                return wide[:, pl.ds(pl.multiple_of(at + k * PIECE, PIECE), PIECE)]

            if lanes:
                turned = [turn(column(0), lanes) if first else kept_image[span, :]]
                turned += [turn(column(k), lanes) for k in (1, 2)]
                kept_image[span, :] = turned[2]
                mask = lane_image < PIECE - lanes
                parts = [jnp.where(mask, turned[k], turned[k + 1]) for k in (0, 1)]
            else:
                parts = [column(0), column(1)]
            for k in (0, 1):
                near, rest = split(parts[k])
                high[parity][span, k * PIECE : (k + 1) * PIECE] = near
                low[parity][span, k * PIECE : (k + 1) * PIECE] = rest

    def multiply(parity, columns=BLOCK):
        for top in range(0, rows, SUB):
            spans = [slice(m * filled + top, m * filled + top + window) for m in range(shifts)]
            near = jnp.concatenate([high[parity][span, :columns] for span in spans], axis=0)
            rest = jnp.concatenate([low[parity][span, :columns] for span in spans], axis=0)
            deep = near.shape[0]
            product = jnp.dot(both_ref[:half, :deep], rest, preferred_element_type=jnp.float32)
            pair = jnp.dot(both_ref[:, :deep], near, preferred_element_type=jnp.float32)
            part[parity][top * GROUP : (top + SUB) * GROUP, :columns] = product + (pair[:half] + pair[half:])

    def keep():
        for first in range(0, rows * GROUP, SUB):
            q = first // SUB % GROUP
            if q:
                kept_part[first : first + SUB, :] = turn(part0[first : first + SUB, :PIECE], q)

    def join(b, parity):
        here, after = part[parity], part[1 - parity]
        begin = pl.multiple_of(b * BLOCK, BLOCK)
        for top in range(0, rows, SUB):
            span = slice(top * GROUP, top * GROUP + SUB)
            totals = [here[span, :PIECE], here[span, PIECE:]]
            for q in range(1, GROUP):
                span = slice(top * GROUP + q * SUB, top * GROUP + (q + 1) * SUB)
                turned = [kept_part[span, :], turn(here[span, PIECE:], q), turn(after[span, :PIECE], q)]
                kept_part[span, :] = turned[2]
                for k in (0, 1):
                    totals[k] = totals[k] + jnp.where(lane_part < PIECE - q, turned[k], turned[k + 1])
            for k in (0, 1):
                at = pl.ds(pl.multiple_of(begin + k * PIECE, PIECE), PIECE)
                result[top : top + SUB, at] = science_ref[top : top + SUB, at] - totals[k]
        store(b).start()

    build(0, 0, first=True)
    build(1, 1)
    multiply(0)
    keep()
    build(2, 0)
    multiply(1)

    @pl.loop(1, blocks // 2)
    def _(p):
        b = p * 2
        join(b - 2, 0)
        build(b + 1, 1)
        multiply(0)
        join(b - 1, 1)
        build(b + 2, 0)
        multiply(1)

    join(blocks - 2, 0)
    multiply(0, PIECE)
    join(blocks - 1, 1)
    for b in range(blocks):
        store(b).wait()


def match(margin, shifts, places, pieces, both, above, below, science, images):
    rows, width = science.shape
    count = len(images)
    slots = images[0].shape[0]
    reach = above.shape[0]
    filled = rows + 2 * reach
    return pl.pallas_call(
        functools.partial(match_kernel, margin, shifts, count, slots, pieces),
        out_shape=jax.ShapeDtypeStruct(science.shape, jnp.float32),
        in_specs=[pl.BlockSpec(memory_space=SMEM)]
        + [pl.BlockSpec(memory_space=VMEM)] * (4 + count),
        out_specs=pl.BlockSpec(memory_space=pl.ANY),
        scratch_shapes=[
            pltpu.VMEM((filled, width + BLOCK + 2 * PIECE), jnp.float32),
            *[pltpu.VMEM((shifts * filled, BLOCK), jnp.bfloat16)] * 4,
            *[pltpu.VMEM((GROUP * rows, BLOCK), jnp.float32)] * 2,
            pltpu.VMEM((shifts * filled, PIECE), jnp.float32),
            pltpu.VMEM((GROUP * rows, PIECE), jnp.float32),
            pltpu.VMEM((rows, width), jnp.float32),
            pltpu.SemaphoreType.DMA((width // BLOCK,)),
        ],
        cost_estimate=pl.CostEstimate(
            flops=6 * GROUP * rows * both.shape[1] * width, transcendentals=0, bytes_accessed=4 * rows * width * 4
        ),
        compiler_params=pltpu.CompilerParams(vmem_limit_bytes=20 << 20),
        name="match",
    )(places, both, above, below, science, *images)


def local(
    science,
    science_var,
    template,
    template_var,
    intersection,
    col_offset,
    basis_row,
    basis_col,
    coef_sets,
    tile_coef,
):
    count = lax.axis_size("visit")
    pieces = intersection.shape[1]
    slots = max(2, pieces // count)
    _, width = science.shape[1:]
    side = basis_row.shape[1]
    margin = (side - 1) // 2
    reach = -(-margin // 8) * 8
    me = lax.axis_index("visit")
    tile_me = lax.axis_index("tile")
    highest = lax.Precision.HIGHEST
    owners = intersection[:, :, 0]
    mine = cut(owners, col_offset, template[0], count, slots)
    got = list(mine)
    for step in flux_steps(count):
        got[step] = lax.ppermute(mine[step], "visit", pairs(step, count))
    mine_var = cut(owners, col_offset, template_var[0], count, slots)
    got_var = list(mine_var)
    for step in near_steps(count) + far_steps(count):
        got_var[step] = lax.ppermute(mine_var[step], "visit", pairs(step, count))

    chosen = lax.dynamic_slice(tile_coef, (me, tile_me), (1, 1))[0, 0]
    coeffs = lax.dynamic_index_in_dim(coef_sets, chosen, 0, keepdims=False)
    taps = jnp.einsum("bc,ba->ca", coeffs[:, None] * basis_col, basis_row, precision=highest)
    power = jnp.sum(taps * taps).reshape(1)
    both, places = bands(taps, SUB + 2 * reach, reach - margin, owners, count, slots)

    head, tail = edges(places, pieces, got, width, reach)
    tiles = lax.axis_size("tile")
    above = lax.ppermute(tail, "tile", [(i, i + 1) for i in range(tiles - 1)])
    below = lax.ppermute(head, "tile", [(i + 1, i) for i in range(tiles - 1)])
    first, second = [0] + near_steps(count), far_steps(count)
    blocks = [got_var[step] for step in first]
    early = early_spread(places, pieces, power, science_var[0], blocks, first, count)
    shifts = -(-side // GROUP)
    difference = match(margin, shifts, places, pieces, both, above, below, science[0], got)
    blocks = [got_var[step] for step in second]
    difference_var = late_spread(places, pieces, power, science_var[0], early, blocks, first, second, count)
    return difference[None], difference_var[None]


def near_steps(count):
    return list(range(1, count // 2))


def far_steps(count):
    far = list(range(count // 2, count))
    return far[:-2] + far[:-3:-1]


def flux_steps(count):
    far = far_steps(count)
    return near_steps(count) + far


def solution(mesh):
    split_spec = P("visit", "tile", None)
    return jax.shard_map(
        local,
        mesh=mesh,
        in_specs=(split_spec,) * 4 + (P(),) * 6,
        out_specs=(split_spec, split_spec),
        check_vma=False,
    )
```
